32 devices in a mesh: group: 8 (over z, y), section: 4 (over x, core).
Axes of the slice: x: 2, y: 2, z: 4, core: 2. Of those that a mesh axis runs over, the one named last changes fastest.
Arguments:
- embed_in: bfloat16 [32, 32, 1792], P(('group', 'section')), may hold values from -6 to 6
- clean_cache: bfloat16 [4, 32, 32, 1792], P('section', 'group'), may hold values from -6 to 6
- lengths: int32 [32, 5], P(('group', 'section')), may hold values from 1 to 24, 32 in all within a row
- patch_layer: int32 [32, 4], P(('group', 'section')), may hold values from 0 to 3
- patch_pos: int32 [32, 4], P(('group', 'section')), may hold values from 0 to 31
- answers: int32 [32, 4, 2], P(('group', 'section')), may hold values from 0 to 77823
- attn_gain: float32 [4, 1792], P('section'), may hold values from 0.5 to 1.5
- w_query: bfloat16 [4, 1792, 1792], P('section', 'group'), may hold values from -0.125 to 0.125
- b_query: float32 [4, 1792], P('section'), may hold values from -3 to 3
- w_keyval: bfloat16 [4, 1792, 512], P('section', 'group'), may hold values from -0.125 to 0.125
- b_key: float32 [4, 256], P('section'), may hold values from -3 to 3
- b_value: float32 [4, 256], P('section'), may hold values from -3 to 3
- w_out: bfloat16 [4, 1792, 1792], P('section', 'group'), may hold values from -0.125 to 0.125
- final_gain: float32 [1792], replicated, may hold values from 0.5 to 1.5
- unembed: bfloat16 [77824, 1792], P(('group', 'section')), may hold values from -0.125 to 0.125
Outputs:
- final_resid: bfloat16 [32, 32, 1792], P(('group', 'section'))
- logit_diff: float32 [32, 4], P(('group', 'section'))
- cell_sums: float32 [4, 24], replicated
The draws below stay inside these ranges and needn't reach their ends.
Inputs may be any that keep to these rules, and one draw needn't show every extreme that they name: Each row holds 4 prompt lengths followed by the padding of its bucket and sums to 32.
All inputs are finite; a program needn't handle non-finite values.
Results may differ from the reference program's by a relative error of at most 0.02.
Values may be sent and summed in bfloat16 or wider, within the bound.
A program may use at most 128 MiB of HBM per device.

```python
import math
import jax
import jax.numpy as jnp
import numpy as np
from jax import lax

D = 1792
HQ = 14
KV = 2
HD = 128
VOCAB = 77824
L = 32
PB = 4
MAXLEN = 24
NB = 32
N_SECTION = 4


def plant(values, stream_key, low, largest):
    dims = values.shape
    index_at = [jax.random.randint(jax.random.fold_in(stream_key, axis), (), 0, dims[axis]) for axis in range(len(dims))]
    values = values.at[tuple(index_at)].set(low)
    longest = dims.index(max(dims))
    index_at[longest] = (index_at[longest] + 1) % dims[longest]
    return values.at[tuple(index_at)].set(largest)


def block_levels(own_key, extent, pieces, smallest, largest):
    gain, own = 1.0, jax.random.fold_in(own_key, 6)
    for dim, parts in pieces:
        heights = jnp.exp(jax.random.uniform(jax.random.fold_in(own, dim), (parts,), jnp.float32, smallest / len(pieces), largest / len(pieces)))
        gain = gain * jnp.repeat(heights, extent[dim] // parts).reshape([-1 if axis == dim else 1 for axis in range(len(extent))])
    return gain


def length_profile(number_of, total, bound, skew):
    loads = [(1 << 20) // math.isqrt(rank ** skew) + 1 for rank in range(2, number_of + 1)]
    surplus, counts = total - bound - (number_of - 1), [1] * (number_of - 1)
    while surplus > 0:
        free = [i for i in range(number_of - 1) if counts[i] < bound]
        whole, remaining = sum([loads[i] for i in free]), surplus
        for i in free:
            extra = min(bound - counts[i], max(1, remaining * loads[i] // whole), surplus)
            counts[i] = counts[i] + extra
            surplus = surplus - extra
    return np.array([bound] + counts)


def ragged_sizes(key, number_of, total, limit, skew):
    if number_of == 2:
        one = jax.random.randint(key, (), max(1, total - limit), min(limit, total - 1) + 1)
        return jnp.stack([one, total - one])
    tallies = jnp.asarray(length_profile(number_of, total, limit, skew), jnp.int32)
    couples = (number_of - 1) // 2
    donor, receiver = tallies[1:1 + 2 * couples:2], tallies[2:2 + 2 * couples:2]
    slack = jnp.minimum(donor - 1, limit - receiver)
    passed = jax.random.randint(jax.random.fold_in(key, 1), (couples,), 0, 1 << 20) % (slack + 1)
    tallies = tallies.at[1:1 + 2 * couples:2].set(donor - passed).at[2:2 + 2 * couples:2].set(receiver + passed)
    return tallies[jax.random.permutation(jax.random.fold_in(key, 2), number_of)]


def centred(rng, extent, deviation, limit, split=(), kind=jnp.bfloat16):
    factor_of = block_levels(rng, extent, split, -0.22, 0.18) if split else 1.0
    entries = jax.random.normal(rng, extent, jnp.float32) * deviation * factor_of
    return jnp.minimum(jnp.maximum(entries, -limit), limit).astype(kind)


def setup_inputs(seed: int = 0) -> dict:
    arg_keys = jax.random.split(jax.random.key(seed), 16)
    return {
        "embed_in": centred(arg_keys[0], (NB, L, D), 1.0, 6.0, ((0, 32),)),
        "clean_cache": centred(arg_keys[1], (N_SECTION, NB, L, D), 1.0, 6.0, ((0, 4), (1, 8))),
        "lengths": jax.vmap(lambda own: ragged_sizes(own, PB + 1, L, MAXLEN, 2))(jax.random.split(arg_keys[2], NB)).reshape((NB, PB + 1)).astype(jnp.int32),
        "patch_layer": plant(jax.random.randint(arg_keys[3], (NB, PB), 0, N_SECTION), jax.random.fold_in(arg_keys[3], 1), 0, N_SECTION - 1).astype(jnp.int32),
        "patch_pos": plant(jax.random.randint(arg_keys[4], (NB, PB), 0, L), jax.random.fold_in(arg_keys[4], 1), 0, L - 1).astype(jnp.int32),
        "answers": plant(jax.random.randint(arg_keys[5], (NB, PB, 2), 0, VOCAB), jax.random.fold_in(arg_keys[5], 1), 0, VOCAB - 1).astype(jnp.int32),
        "attn_gain": jnp.clip(1.0 + 0.1 * jax.random.normal(arg_keys[6], (N_SECTION, D), jnp.float32), 0.5, 1.5),
        "w_query": centred(arg_keys[7], (N_SECTION, D, HQ * HD), D ** -0.5, 0.125, ((0, 4), (1, 8))),
        "b_query": centred(arg_keys[8], (N_SECTION, HQ * HD), 0.5, 3.0, ((0, 4),), jnp.float32),
        "w_keyval": centred(arg_keys[9], (N_SECTION, D, 2 * KV * HD), D ** -0.5, 0.125, ((0, 4), (1, 8))),
        "b_key": centred(arg_keys[10], (N_SECTION, KV * HD), 0.5, 3.0, ((0, 4),), jnp.float32),
        "b_value": centred(arg_keys[11], (N_SECTION, KV * HD), 0.5, 3.0, ((0, 4),), jnp.float32),
        "w_out": centred(arg_keys[12], (N_SECTION, HQ * HD, D), (HQ * HD) ** -0.5, 0.125, ((0, 4), (1, 8))),
        "final_gain": jnp.clip(1.0 + 0.1 * jax.random.normal(arg_keys[13], (D,), jnp.float32), 0.5, 1.5),
        "unembed": centred(arg_keys[14], (VOCAB, D), D ** -0.5, 0.125, ((0, 32),)),
    }


epsilon = 1e-06
rope_base = 1000000.0

def rmsnorm(hidden, norm_gain):
    residual = hidden.astype(jnp.float32)
    scaled = residual * lax.rsqrt(lax.optimization_barrier(jnp.mean(residual * residual, axis=-1, keepdims=True)) + epsilon)
    return (scaled * norm_gain).astype(jnp.bfloat16)

def rotary(heads, position):
    half_dim = heads.shape[-1] // 2
    frequency = jnp.exp(jnp.arange(half_dim, dtype=jnp.float32) * (-math.log(rope_base) / half_dim))
    angles = position.astype(jnp.float32)[:, None] * frequency[None, :]
    cosine = jnp.cos(angles)[:, None, :]
    sinus = jnp.sin(angles)[:, None, :]
    front_half = heads[..., :half_dim]
    back_half = heads[..., half_dim:]
    return jnp.concatenate([front_half * cosine - back_half * sinus, back_half * cosine + front_half * sinus], axis=-1)

def bucket_layout(lengths_rows, seq_len):
    end_rows = jnp.cumsum(lengths_rows, axis=-1).astype(jnp.int32)
    starts = (end_rows - lengths_rows).astype(jnp.int32)
    row_ids = jnp.arange(seq_len, dtype=jnp.int32)
    segment = lax.optimization_barrier(jnp.sum((row_ids[:, None] >= end_rows[..., None, :]).astype(jnp.int32), axis=-1)).astype(jnp.int32)
    slots = jnp.arange(lengths_rows.shape[-1], dtype=jnp.int32)
    member = segment[..., :, None] == slots
    position = (row_ids - lax.optimization_barrier(jnp.sum(jnp.where(member, starts[..., None, :], 0), axis=-1))).astype(jnp.int32)
    return (segment, position, starts)

def patch_hits(starts, lengths_rows, layers, offsets, layer_now, seq_len):
    prompts = layers.shape[-1]
    target = (starts[..., :prompts] + offsets % lengths_rows[..., :prompts]).astype(jnp.int32)
    row_ids = jnp.arange(seq_len, dtype=jnp.int32)
    return jnp.any((row_ids[:, None] == target[..., None, :]) & (layers[..., None, :] == layer_now), axis=-1)

def attention_layer(hidden, norm_gain, query_weight, query_bias, keyval_weight, key_bias, value_bias, output_weight, segment, position):
    count_rows = hidden.shape[0]
    normed = rmsnorm(hidden, norm_gain)
    queries = jnp.dot(normed, query_weight, preferred_element_type=jnp.float32) + query_bias
    keyval = jnp.dot(normed, keyval_weight, preferred_element_type=jnp.float32)
    width_kv = keyval.shape[1] // 2
    keys_rot = rotary((keyval[:, :width_kv] + key_bias).reshape(count_rows, KV, HD), position).astype(jnp.bfloat16)
    values_all = (keyval[:, width_kv:] + value_bias).reshape(count_rows, KV, HD).astype(jnp.bfloat16)
    queries_rot = rotary(queries.reshape(count_rows, HQ, HD), position).astype(jnp.bfloat16)
    queries_rot = queries_rot.reshape(count_rows, KV, HQ // KV, HD)
    scores = jnp.einsum('qgrd,kgd->grqk', queries_rot.astype(jnp.float32), keys_rot.astype(jnp.float32)) * HD ** (-0.5)
    row_ids = jnp.arange(count_rows, dtype=jnp.int32)
    allowed = (segment[:, None] == segment[None, :]) & (row_ids[None, :] <= row_ids[:, None])
    scores = jnp.where(allowed, scores, -1e+30)
    weights = jax.nn.softmax(scores, axis=-1).astype(jnp.bfloat16)
    attended = jnp.einsum('grqk,kgd->qgrd', weights.astype(jnp.float32), values_all.astype(jnp.float32))
    attended = attended.astype(jnp.bfloat16).reshape(count_rows, HQ * HD)
    updated = hidden.astype(jnp.float32) + jnp.dot(attended, output_weight, preferred_element_type=jnp.float32)
    return updated.astype(jnp.bfloat16)

def reference(embed_in, clean_cache, lengths, patch_layer, patch_pos, answers, attn_gain, w_query, b_query, w_keyval, b_key, b_value, w_out, final_gain, unembed):
    segment, position, starts = bucket_layout(lengths, L)

    def one_bucket(items):
        hidden, clean, seg_row, pos_row, start_row, length_row, layer_row, offset_row = items
        for layer_now in range(N_SECTION):
            patched = patch_hits(start_row, length_row, layer_row, offset_row, layer_now, L)
            hidden = jnp.where(patched[:, None], clean[layer_now], hidden)
            hidden = attention_layer(hidden, attn_gain[layer_now], w_query[layer_now], b_query[layer_now], w_keyval[layer_now], b_key[layer_now], b_value[layer_now], w_out[layer_now], seg_row, pos_row)
        return hidden
    final_resid = lax.map(one_bucket, (embed_in, jnp.swapaxes(clean_cache, 0, 1), segment, position, starts, lengths, patch_layer, patch_pos))
    prompts = patch_layer.shape[1]
    last_rows = (starts[:, :prompts] + lengths[:, :prompts] - 1).astype(jnp.int32)
    picked = jnp.take_along_axis(final_resid, last_rows[:, :, None], axis=1)
    readout = rmsnorm(picked, final_gain).astype(jnp.float32)
    right_rows = unembed[answers[..., 0]].astype(jnp.float32)
    wrong_rows = unembed[answers[..., 1]].astype(jnp.float32)
    logit_diff = lax.optimization_barrier(jnp.sum(readout * right_rows, axis=-1)) - lax.optimization_barrier(jnp.sum(readout * wrong_rows, axis=-1))
    offsets = lengths[:, :prompts] - 1 - patch_pos % lengths[:, :prompts]
    cell_ids = (patch_layer * MAXLEN + offsets).astype(jnp.int32).reshape(-1)
    onehot = (cell_ids[:, None] == jnp.arange(N_SECTION * MAXLEN, dtype=jnp.int32)[None, :]).astype(jnp.float32)
    cell_sums = jnp.dot(logit_diff.reshape(-1), onehot, precision=lax.Precision.HIGHEST).reshape(N_SECTION, MAXLEN)
    return (final_resid, logit_diff, cell_sums)
```

```python
import functools
import math

import jax
import jax.numpy as jnp
from jax import lax
from jax.experimental import pallas as pl
from jax.experimental.pallas import tpu as pltpu
from jax.sharding import PartitionSpec as P

HD = 128
MAXLEN = 24
EPS = 1e-06
ROPE_BASE = 1000000.0
MESH = pl.DeviceIdType.MESH
TILE = 256
STAT = 8


def rms(rows, gain):
    x = rows.astype(jnp.float32)
    scaled = x * lax.rsqrt(jnp.mean(x * x, axis=-1, keepdims=True) + EPS)
    return (scaled * gain).astype(jnp.bfloat16)


def ring_group(place, n):
    late = place // (n // 2)
    return (1 - late) * 2 * place + late * (2 * (n - 1 - place) + 1)


def window_kernel(
    n,
    ns,
    ring,
    embed,
    wq,
    wkv,
    wo,
    terms,
    clean,
    hit,
    mask,
    cosine,
    sinus,
    gain,
    bq,
    bk,
    bv,
    final_gain,
    pick,
    cells,
    rows_out,
    stats_out,
    wq_all,
    wkv_all,
    wo_all,
    h_in,
    h_out,
    normed,
    q_rot,
    k_rot,
    v_all,
    att,
    term_buf,
    stat,
    w_send,
    w_recv,
    w_local,
    e_send,
    e_recv,
    t_send,
    t_recv,
    t_local,
    h_send,
    h_recv,
    r_send,
    r_recv,
    s_send,
    s_recv,
):
    g = lax.axis_index("group")
    s = lax.axis_index("section")
    total = n * ns
    me = g * ns + s
    last = ns - 1
    bucket = embed.shape[0]
    d = embed.shape[1]
    width = wq_all.shape[1]
    kvw = wkv_all.shape[1] // 2
    kv_heads = kvw // HD
    heads = width // HD
    per = heads // kv_heads

    barrier = pltpu.get_barrier_semaphore()

    def greet(i, c):
        t = lax.rem(me + i, total)
        pl.semaphore_signal(barrier, inc=1, device_id=(t // ns, lax.rem(t, ns)), device_id_type=MESH)
        return c

    lax.fori_loop(1, total, greet, 0)
    pl.semaphore_wait(barrier, total - 1)

    ins = (wq, wkv, wo)
    alls = (wq_all, wkv_all, wo_all)
    shard = wq.shape[0]
    if ring:
        odd = lax.rem(g, 2)
        place = (1 - odd) * (g // 2) + odd * (n - 1 - g // 2)
        right = ring_group(lax.rem(place + 1, n), n)
        left = ring_group(lax.rem(place + n - 1, n), n)
        half = n // 2

        def rows_of(step, way):
            at = lax.rem(place + n - step, n) if way == 0 else lax.rem(place + step, n)
            return pl.ds(pl.multiple_of(ring_group(at, n) * shard, shard), shard)

        def hop(step, way, a):
            rows = rows_of(step, way)
            src = ins[a] if step == 0 else alls[a].at[rows]
            return pltpu.make_async_remote_copy(
                src_ref=src,
                dst_ref=alls[a].at[rows],
                send_sem=w_send.at[way, step, a],
                recv_sem=w_recv.at[way, step, a],
                device_id=((right, left)[way], s),
                device_id_type=MESH,
            )

        def used(step, way, a):
            if step < half - 1:
                return True
            return (a == 0) if way == 0 else (a != 0)

        for a in range(3):
            for way in range(2):
                if used(0, way, a):
                    hop(0, way, a).start()
        own = pl.ds(pl.multiple_of(g * shard, shard), shard)
    else:
        own = pl.ds(0, shard)
    local = [
        pltpu.make_async_copy(ins[a], alls[a].at[own], w_local.at[a]) for a in range(3)
    ]
    for copy in local:
        copy.start()

    own_rows = pl.ds(pl.multiple_of(s * bucket, bucket), bucket)
    e_out = pltpu.make_async_remote_copy(
        src_ref=embed,
        dst_ref=h_in.at[own_rows],
        send_sem=e_send,
        recv_sem=e_recv.at[s],
        device_id=(g, 0),
        device_id_type=MESH,
    )
    e_own = pltpu.make_async_copy(embed, h_in.at[own_rows], e_send)

    @pl.when(s != 0)
    def _():
        e_out.start()

    @pl.when(s == 0)
    def _():
        e_own.start()

    def term_copy(i, slot):
        t = lax.rem(g + i, n)
        return pltpu.make_async_remote_copy(
            src_ref=terms.at[t],
            dst_ref=term_buf.at[slot],
            send_sem=t_send.at[i],
            recv_sem=t_recv.at[slot],
            device_id=(t, last),
            device_id_type=MESH,
        )

    def send_term(i, c):
        term_copy(i, me).start()
        return c

    t_own = pltpu.make_async_copy(terms.at[g], term_buf.at[me], t_local)

    @pl.when(s == last)
    def _():
        t_own.start()

    @pl.when(s != last)
    def _():
        term_copy(0, me).start()

    lax.fori_loop(1, n, send_term, 0)

    if ring:
        for step in range(1, half):
            for a in range(3):
                for way in range(2):
                    hop(step - 1, way, a).wait_recv()
                    if used(step, way, a):
                        hop(step, way, a).start()
        for a in range(3):
            for way in range(2):
                if used(half - 1, way, a):
                    hop(half - 1, way, a).wait_recv()
        for step in range(half):
            for a in range(3):
                for way in range(2):
                    if used(step, way, a):
                        hop(step, way, a).wait_send()
    for copy in local:
        copy.wait()

    h_copy = pltpu.make_async_remote_copy(
        src_ref=h_out,
        dst_ref=h_in,
        send_sem=h_send,
        recv_sem=h_recv,
        device_id=(g, lax.rem(s + 1, ns)),
        device_id_type=MESH,
    )

    @pl.when(s == 0)
    def _():
        e_own.wait()
        for i in range(1, ns):
            rows = pl.ds(i * bucket, bucket)
            pltpu.make_async_remote_copy(
                src_ref=embed,
                dst_ref=h_in.at[rows],
                send_sem=e_send,
                recv_sem=e_recv.at[i],
                device_id=(g, 0),
                device_id_type=MESH,
            ).wait_recv()

    @pl.when(s != 0)
    def _():
        e_out.wait_send()
        h_copy.wait_recv()

    h_in[...] = jnp.where(hit[...] > 0, clean[...], h_in[...])
    normed[...] = rms(h_in[...], gain[...])
    cos_t = cosine[...]
    sin_t = sinus[...]

    def rotate(x):
        return (x * cos_t + pltpu.roll(x, HD // 2, 1) * sin_t).astype(jnp.bfloat16)

    keys = jnp.dot(normed[...], wkv_all[:, :kvw], preferred_element_type=jnp.float32) + bk[...]
    for k in range(kv_heads):
        k_rot[k] = rotate(keys[:, k * HD : (k + 1) * HD])
    values = jnp.dot(normed[...], wkv_all[:, kvw:], preferred_element_type=jnp.float32) + bv[...]
    v_all[...] = values.astype(jnp.bfloat16)

    def query_tile(t, c):
        cols = pl.ds(pl.multiple_of(t * TILE, TILE), TILE)
        q = jnp.dot(normed[...], wq_all[:, cols], preferred_element_type=jnp.float32) + bq[:, cols]
        for k in range(TILE // HD):
            q_rot[t * (TILE // HD) + k] = rotate(q[:, k * HD : (k + 1) * HD])
        return c

    lax.fori_loop(0, width // TILE, query_tile, 0)
    rows_all = h_in.shape[0]
    open_ = mask[...] > 0
    for h in range(heads):
        k = h // per
        sc = lax.dot_general(
            q_rot[h], k_rot[k], (((1,), (1,)), ((), ())), preferred_element_type=jnp.float32
        ) * HD ** (-0.5)
        sc = jnp.where(open_, sc, -1e30)
        ex = jnp.exp(sc - jnp.max(sc, axis=-1, keepdims=True))
        w = (ex / jnp.sum(ex, axis=-1, keepdims=True)).astype(jnp.bfloat16)
        att[:, h * HD : (h + 1) * HD] = jnp.dot(
            w, v_all[:, k * HD : (k + 1) * HD], preferred_element_type=jnp.float32
        ).astype(jnp.bfloat16)

    def out_tile(t, c):
        cols = pl.ds(pl.multiple_of(t * TILE, TILE), TILE)
        up = jnp.dot(att[...], wo_all[:, cols], preferred_element_type=jnp.float32)
        h_out[:, cols] = (h_in[:, cols].astype(jnp.float32) + up).astype(jnp.bfloat16)
        return c

    lax.fori_loop(0, d // TILE, out_tile, 0)

    @pl.when(s != last)
    def _():
        h_copy.start()

    def row_copy(i):
        return pltpu.make_async_remote_copy(
            src_ref=h_out.at[pl.ds(i * bucket, bucket)],
            dst_ref=rows_out,
            send_sem=r_send.at[i],
            recv_sem=r_recv,
            device_id=(g, i),
            device_id_type=MESH,
        )

    def stat_copy(i, slot):
        t = lax.rem(me + i, total)
        return pltpu.make_async_remote_copy(
            src_ref=stat,
            dst_ref=stats_out.at[slot],
            send_sem=s_send.at[i],
            recv_sem=s_recv.at[slot],
            device_id=(t // ns, lax.rem(t, ns)),
            device_id_type=MESH,
        )

    def wait_stat(slot):
        stat_copy(1, slot).wait_recv()

    @pl.when(s == last)
    def _():
        for i in range(last):
            row_copy(i).start()
        row_own = pltpu.make_async_copy(
            h_out.at[pl.ds(last * bucket, bucket)], rows_out, r_send.at[last]
        )
        row_own.start()

        t_own.wait()

        def take_term(i, c):
            term_copy(1, lax.rem(me + i, total)).wait_recv()
            return c

        lax.fori_loop(1, total, take_term, 0)

        def add_term(i, acc):
            return acc + term_buf[i].astype(jnp.float32)

        diff_rows = lax.fori_loop(1, total, add_term, term_buf[0].astype(jnp.float32))
        picked = jnp.dot(pick[...], h_out[...], preferred_element_type=jnp.float32)
        readout = rms(picked, final_gain[...]).astype(jnp.float32)
        diffs = jnp.sum(readout * diff_rows, axis=-1, keepdims=True)
        stat[STAT:, :] = jnp.broadcast_to(diffs, (stat.shape[0] - STAT, HD))
        stat[:STAT, :] = jnp.broadcast_to(
            jnp.sum(diffs * cells[...], axis=0, keepdims=True), (STAT, HD)
        )
        s_own = pltpu.make_async_copy(stat, stats_out.at[g], s_send.at[0])
        s_own.start()

        def send_stat(i, c):
            stat_copy(i, g).start()
            return c

        lax.fori_loop(1, total, send_stat, 0)

        def others(i, c):
            wait_stat(lax.rem(g + i, n))
            return c

        lax.fori_loop(1, n, others, 0)

        def sent(i, c):
            stat_copy(i, g).wait_send()
            return c

        lax.fori_loop(1, total, sent, 0)
        s_own.wait()
        row_own.wait()
        for i in range(last):
            row_copy(i).wait_send()

    @pl.when(s != last)
    def _():
        h_copy.wait_send()
        term_copy(0, me).wait_send()
        row_copy(0).wait_recv()

        def every(i, c):
            wait_stat(i)
            return c

        lax.fori_loop(0, n, every, 0)

    def term_sent(i, c):
        term_copy(i, me).wait_send()
        return c

    lax.fori_loop(1, n, term_sent, 0)


def bucket_layout(lengths_rows, seq_len):
    end_rows = jnp.cumsum(lengths_rows, axis=-1).astype(jnp.int32)
    starts = (end_rows - lengths_rows).astype(jnp.int32)
    row_ids = jnp.arange(seq_len, dtype=jnp.int32)
    segment = jnp.sum((row_ids[:, None] >= end_rows[..., None, :]).astype(jnp.int32), axis=-1)
    slots = jnp.arange(lengths_rows.shape[-1], dtype=jnp.int32)
    member = segment[..., :, None] == slots
    position = row_ids - jnp.sum(jnp.where(member, starts[..., None, :], 0), axis=-1)
    return (segment, position, starts)


def per_device(
    n,
    ns,
    embed_in,
    clean_cache,
    lengths,
    patch_layer,
    patch_pos,
    answers,
    attn_gain,
    w_query,
    b_query,
    w_keyval,
    b_key,
    b_value,
    w_out,
    final_gain,
    unembed,
):
    g = lax.axis_index("group")
    s = lax.axis_index("section")
    seq_len, d = embed_in.shape[1:]
    prompts = patch_layer.shape[1]
    entries = lengths.shape[1]
    width = w_query.shape[2]
    kvw = b_key.shape[1]
    rows_all = ns * seq_len
    total = n * ns

    packed = jnp.concatenate(
        [lengths, patch_layer, patch_pos, answers.reshape(1, 2 * prompts)], axis=1
    )
    table = lax.all_gather(packed, ("group", "section"), axis=0, tiled=True)
    at = entries + 2 * prompts
    answer_ids = table[:, at:].reshape(total * prompts, 2)
    mine = lax.dynamic_slice_in_dim(table, g * ns, ns, 0)
    lens = mine[:, :entries]
    layers = mine[:, entries : entries + prompts]
    offsets = mine[:, entries + prompts : at]

    vocab_ids = (g * ns + s) * unembed.shape[0] + jnp.arange(unembed.shape[0], dtype=jnp.int32)
    choosing = (answer_ids[:, 0:1] == vocab_ids[None, :]).astype(jnp.bfloat16) - (
        answer_ids[:, 1:2] == vocab_ids[None, :]
    ).astype(jnp.bfloat16)
    terms = jnp.dot(choosing, unembed, preferred_element_type=jnp.float32).astype(jnp.bfloat16)
    terms = terms.reshape(n, ns * prompts, d)

    segment, position, starts = bucket_layout(lens, seq_len)
    row_ids = jnp.arange(seq_len, dtype=jnp.int32)
    folded = offsets % lens[:, :prompts]
    target = starts[:, :prompts] + folded
    hit = jnp.any(
        (row_ids[:, None] == target[:, None, :]) & (layers[:, None, :] == s), axis=-1
    )
    hit = hit.reshape(rows_all, 1).astype(jnp.float32)
    ident = (segment + jnp.arange(ns, dtype=jnp.int32)[:, None] * entries).reshape(rows_all)
    all_rows = jnp.arange(rows_all, dtype=jnp.int32)
    mask = (
        (ident[:, None] == ident[None, :]) & (all_rows[None, :] <= all_rows[:, None])
    ).astype(jnp.float32)
    half = HD // 2
    frequency = jnp.exp(jnp.arange(half, dtype=jnp.float32) * (-math.log(ROPE_BASE) / half))
    angles = position.reshape(rows_all, 1).astype(jnp.float32) * frequency[None, :]
    cos_h = jnp.cos(angles)
    sin_h = jnp.sin(angles)
    cosine = jnp.concatenate([cos_h, cos_h], axis=1)
    sinus = jnp.concatenate([-sin_h, sin_h], axis=1)

    ends = starts[:, :prompts] + lens[:, :prompts] - 1
    last_rows = (ends + jnp.arange(ns, dtype=jnp.int32)[:, None] * seq_len).reshape(-1)
    pick = (last_rows[:, None] == all_rows[None, :]).astype(jnp.bfloat16)
    distance = lens[:, :prompts] - 1 - folded
    cell_ids = (layers * MAXLEN + distance).reshape(-1)
    cells = (cell_ids[:, None] == jnp.arange(HD, dtype=jnp.int32)[None, :]).astype(jnp.float32)

    wq, wkv, wo = w_query[0], w_keyval[0], w_out[0]
    ring = n % 2 == 0 and n > 2 and wq.shape[0] % 16 == 0
    if not ring:
        wq, wkv, wo = (lax.all_gather(w, "group", axis=0, tiled=True) for w in (wq, wkv, wo))
    hops = max(n // 2, 1) if ring else 1
    any_ = pl.BlockSpec(memory_space=pl.ANY)
    vmem = pl.BlockSpec(memory_space=pltpu.VMEM)
    dma = pltpu.SemaphoreType.DMA
    stat_rows = STAT + ns * prompts
    rows, stats = pl.pallas_call(
        functools.partial(window_kernel, n, ns, ring),
        out_shape=(
            jax.ShapeDtypeStruct((seq_len, d), jnp.bfloat16),
            jax.ShapeDtypeStruct((n, stat_rows, HD), jnp.float32),
        ),
        in_specs=[any_] * 5 + [vmem] * 12,
        out_specs=(vmem, vmem),
        scratch_shapes=[
            pltpu.VMEM((d, width), jnp.bfloat16),
            pltpu.VMEM((d, 2 * kvw), jnp.bfloat16),
            pltpu.VMEM((width, d), jnp.bfloat16),
            pltpu.VMEM((rows_all, d), jnp.bfloat16),
            pltpu.VMEM((rows_all, d), jnp.bfloat16),
            pltpu.VMEM((rows_all, d), jnp.bfloat16),
            pltpu.VMEM((width // HD, rows_all, HD), jnp.bfloat16),
            pltpu.VMEM((kvw // HD, rows_all, HD), jnp.bfloat16),
            pltpu.VMEM((rows_all, kvw), jnp.bfloat16),
            pltpu.VMEM((rows_all, width), jnp.bfloat16),
            pltpu.VMEM((total, ns * prompts, d), jnp.bfloat16),
            pltpu.VMEM((stat_rows, HD), jnp.float32),
            dma((2, hops, 3)),
            dma((2, hops, 3)),
            dma((3,)),
            dma,
            dma((ns,)),
            dma((n,)),
            dma((total,)),
            dma,
            dma,
            dma,
            dma((ns,)),
            dma,
            dma((total,)),
            dma((n,)),
        ],
        compiler_params=pltpu.CompilerParams(
            collective_id=0, has_side_effects=True, vmem_limit_bytes=60 * 1024 * 1024
        ),
    )(
        embed_in[0],
        wq,
        wkv,
        wo,
        terms,
        clean_cache[0].reshape(rows_all, d),
        hit,
        mask,
        cosine,
        sinus,
        attn_gain,
        b_query,
        b_key,
        b_value,
        final_gain[None, :],
        pick,
        cells,
    )
    totals = jnp.sum(stats[:, 0, :], axis=0)[: ns * MAXLEN].reshape(ns, MAXLEN)
    group_diffs = lax.dynamic_slice_in_dim(stats, g, 1, 0)[0, STAT:, 0]
    diffs = lax.dynamic_slice_in_dim(group_diffs, s * prompts, prompts, 0)
    return (rows[None], diffs[None, :], totals)


def solution(mesh):
    placed = (
        P(("group", "section"), None, None),
        P("section", "group", None, None),
        P(("group", "section"), None),
        P(("group", "section"), None),
        P(("group", "section"), None),
        P(("group", "section"), None, None),
        P("section", None),
        P("section", "group", None),
        P("section", None),
        P("section", "group", None),
        P("section", None),
        P("section", None),
        P("section", "group", None),
        P(),
        P(("group", "section"), None),
    )
    return jax.shard_map(
        functools.partial(per_device, mesh.shape["group"], mesh.shape["section"]),
        mesh=mesh,
        in_specs=placed,
        out_specs=(P(("group", "section"), None, None), P(("group", "section"), None), P()),
        check_vma=False,
    )
```

```python
import functools
import math

import jax
import jax.numpy as jnp
from jax import lax
from jax.experimental import pallas as pl
from jax.experimental.pallas import tpu as pltpu
from jax.sharding import PartitionSpec as P

HD = 128
MAXLEN = 24
EPS = 1e-06
ROPE_BASE = 1000000.0
MESH = pl.DeviceIdType.MESH
TILE = 256
STAT = 8


def rms(rows, gain):
    x = rows.astype(jnp.float32)
    scaled = x * lax.rsqrt(jnp.mean(x * x, axis=-1, keepdims=True) + EPS)
    return (scaled * gain).astype(jnp.bfloat16)


def share_kernel(n, ns, tile, out, send, recv, local):
    g = lax.axis_index("group")
    s = lax.axis_index("section")
    total = n * ns
    me = g * ns + s
    greet_all(me, ns, total)

    def copy(i, slot):
        t = lax.rem(me + i, total)
        return pltpu.make_async_remote_copy(
            src_ref=tile,
            dst_ref=out.at[slot],
            send_sem=send.at[i],
            recv_sem=recv.at[slot],
            device_id=(t // ns, lax.rem(t, ns)),
            device_id_type=MESH,
        )

    def start(i, c):
        copy(i, me).start()
        return c

    def finish(i, c):
        copy(i, lax.rem(me + i, total)).wait_recv()
        return c

    def sent(i, c):
        copy(i, me).wait_send()
        return c

    lax.fori_loop(1, total, start, 0)
    own = pltpu.make_async_copy(tile, out.at[me], local)
    own.start()
    lax.fori_loop(1, total, finish, 0)
    lax.fori_loop(1, total, sent, 0)
    own.wait()


def share(packed, n, ns):
    total = n * ns
    vmem = pl.BlockSpec(memory_space=pltpu.VMEM)
    dma = pltpu.SemaphoreType.DMA
    return pl.pallas_call(
        functools.partial(share_kernel, n, ns),
        out_shape=jax.ShapeDtypeStruct((total,) + packed.shape, packed.dtype),
        in_specs=[vmem],
        out_specs=vmem,
        scratch_shapes=[dma((total,)), dma((total,)), dma],
        compiler_params=pltpu.CompilerParams(collective_id=1, has_side_effects=True),
    )(packed)


def greet_all(me, ns, total):
    barrier = pltpu.get_barrier_semaphore()

    def greet(i, c):
        t = lax.rem(me + i, total)
        pl.semaphore_signal(barrier, inc=1, device_id=(t // ns, lax.rem(t, ns)), device_id_type=MESH)
        return c

    lax.fori_loop(1, total, greet, 0)
    pl.semaphore_wait(barrier, total - 1)


def ring_group(place, n):
    late = place // (n // 2)
    return (1 - late) * 2 * place + late * (2 * (n - 1 - place) + 1)


def window_kernel(
    n,
    ns,
    ring,
    embed,
    wq,
    wkv,
    wo,
    unembed,
    choose,
    clean,
    hit,
    mask,
    cosine,
    sinus,
    gain,
    bq,
    bk,
    bv,
    final_gain,
    pick,
    cells,
    rows_out,
    totals_out,
    diffs_out,
    wq_all,
    wkv_all,
    wo_all,
    h_in,
    h_out,
    normed,
    q_rot,
    k_rot,
    v_all,
    att,
    term_buf,
    stat,
    stats_all,
    shard_rows,
    terms,
    u_sem,
    w_send,
    w_recv,
    w_local,
    e_send,
    e_recv,
    t_send,
    t_recv,
    t_local,
    h_send,
    h_recv,
    r_send,
    r_recv,
    s_send,
    s_recv,
):
    g = lax.axis_index("group")
    s = lax.axis_index("section")
    total = n * ns
    me = g * ns + s
    last = ns - 1
    bucket = embed.shape[0]
    d = embed.shape[1]
    width = wq_all.shape[1]
    kvw = wkv_all.shape[1] // 2
    kv_heads = kvw // HD
    heads = width // HD
    per = heads // kv_heads

    greet_all(me, ns, total)
    vocab = pltpu.make_async_copy(unembed, shard_rows, u_sem)
    vocab.start()

    ins = (wq, wkv, wo)
    alls = (wq_all, wkv_all, wo_all)
    shard = wq.shape[0]
    if ring:
        odd = lax.rem(g, 2)
        place = (1 - odd) * (g // 2) + odd * (n - 1 - g // 2)
        right = ring_group(lax.rem(place + 1, n), n)
        left = ring_group(lax.rem(place + n - 1, n), n)
        half = n // 2

        def rows_of(step, way):
            at = lax.rem(place + n - step, n) if way == 0 else lax.rem(place + step, n)
            return pl.ds(pl.multiple_of(ring_group(at, n) * shard, shard), shard)

        def hop(step, way, a):
            rows = rows_of(step, way)
            src = ins[a] if step == 0 else alls[a].at[rows]
            return pltpu.make_async_remote_copy(
                src_ref=src,
                dst_ref=alls[a].at[rows],
                send_sem=w_send.at[way, step, a],
                recv_sem=w_recv.at[way, step, a],
                device_id=((right, left)[way], s),
                device_id_type=MESH,
            )

        def used(step, way, a):
            if step < half - 1:
                return True
            return (a == 0) if way == 0 else (a != 0)

        for a in range(3):
            for way in range(2):
                if used(0, way, a):
                    hop(0, way, a).start()
        own = pl.ds(pl.multiple_of(g * shard, shard), shard)
    else:
        own = pl.ds(0, shard)
    local = [
        pltpu.make_async_copy(ins[a], alls[a].at[own], w_local.at[a]) for a in range(3)
    ]
    for copy in local:
        copy.start()

    own_rows = pl.ds(pl.multiple_of(s * bucket, bucket), bucket)
    e_out = pltpu.make_async_remote_copy(
        src_ref=embed,
        dst_ref=h_in.at[own_rows],
        send_sem=e_send,
        recv_sem=e_recv.at[s],
        device_id=(g, 0),
        device_id_type=MESH,
    )
    e_own = pltpu.make_async_copy(embed, h_in.at[own_rows], e_send)

    @pl.when(s != 0)
    def _():
        e_out.start()

    @pl.when(s == 0)
    def _():
        e_own.start()

    vocab.wait()
    block = terms.shape[1]

    def term_tile(t, c):
        cols = pl.ds(pl.multiple_of(t * TILE, TILE), TILE)
        part = jnp.dot(choose[...], shard_rows[:, cols], preferred_element_type=jnp.float32)
        part = part.astype(jnp.bfloat16)
        for k in range(n):
            terms[k, :, cols] = part[k * block : (k + 1) * block]
        return c

    lax.fori_loop(0, d // TILE, term_tile, 0)

    def term_copy(i, slot):
        t = lax.rem(g + i, n)
        return pltpu.make_async_remote_copy(
            src_ref=terms.at[t],
            dst_ref=term_buf.at[slot],
            send_sem=t_send.at[i],
            recv_sem=t_recv.at[slot],
            device_id=(t, last),
            device_id_type=MESH,
        )

    def send_term(i, c):
        term_copy(i, me).start()
        return c

    t_own = pltpu.make_async_copy(terms.at[g], term_buf.at[me], t_local)

    @pl.when(s == last)
    def _():
        t_own.start()

    @pl.when(s != last)
    def _():
        term_copy(0, me).start()

    lax.fori_loop(1, n, send_term, 0)

    if ring:
        for step in range(1, half):
            for a in range(3):
                for way in range(2):
                    hop(step - 1, way, a).wait_recv()
                    if used(step, way, a):
                        hop(step, way, a).start()
        for a in range(3):
            for way in range(2):
                if used(half - 1, way, a):
                    hop(half - 1, way, a).wait_recv()
        for step in range(half):
            for a in range(3):
                for way in range(2):
                    if used(step, way, a):
                        hop(step, way, a).wait_send()
    for copy in local:
        copy.wait()

    h_copy = pltpu.make_async_remote_copy(
        src_ref=h_out,
        dst_ref=h_in,
        send_sem=h_send,
        recv_sem=h_recv,
        device_id=(g, lax.rem(s + 1, ns)),
        device_id_type=MESH,
    )

    @pl.when(s == 0)
    def _():
        e_own.wait()
        for i in range(1, ns):
            rows = pl.ds(i * bucket, bucket)
            pltpu.make_async_remote_copy(
                src_ref=embed,
                dst_ref=h_in.at[rows],
                send_sem=e_send,
                recv_sem=e_recv.at[i],
                device_id=(g, 0),
                device_id_type=MESH,
            ).wait_recv()

    @pl.when(s != 0)
    def _():
        e_out.wait_send()
        h_copy.wait_recv()

    h_in[...] = jnp.where(hit[...] > 0, clean[...], h_in[...])
    normed[...] = rms(h_in[...], gain[...])
    cos_t = cosine[...]
    sin_t = sinus[...]

    def rotate(x):
        return (x * cos_t + pltpu.roll(x, HD // 2, 1) * sin_t).astype(jnp.bfloat16)

    keys = jnp.dot(normed[...], wkv_all[:, :kvw], preferred_element_type=jnp.float32) + bk[...]
    for k in range(kv_heads):
        k_rot[k] = rotate(keys[:, k * HD : (k + 1) * HD])
    values = jnp.dot(normed[...], wkv_all[:, kvw:], preferred_element_type=jnp.float32) + bv[...]
    v_all[...] = values.astype(jnp.bfloat16)

    def query_tile(t, c):
        cols = pl.ds(pl.multiple_of(t * TILE, TILE), TILE)
        q = jnp.dot(normed[...], wq_all[:, cols], preferred_element_type=jnp.float32) + bq[:, cols]
        for k in range(TILE // HD):
            q_rot[t * (TILE // HD) + k] = rotate(q[:, k * HD : (k + 1) * HD])
        return c

    lax.fori_loop(0, width // TILE, query_tile, 0)
    rows_all = h_in.shape[0]
    open_ = mask[...] > 0
    for h in range(heads):
        k = h // per
        sc = lax.dot_general(
            q_rot[h], k_rot[k], (((1,), (1,)), ((), ())), preferred_element_type=jnp.float32
        ) * HD ** (-0.5)
        sc = jnp.where(open_, sc, -1e30)
        ex = jnp.exp(sc - jnp.max(sc, axis=-1, keepdims=True))
        w = (ex / jnp.sum(ex, axis=-1, keepdims=True)).astype(jnp.bfloat16)
        att[:, h * HD : (h + 1) * HD] = jnp.dot(
            w, v_all[:, k * HD : (k + 1) * HD], preferred_element_type=jnp.float32
        ).astype(jnp.bfloat16)

    def out_tile(t, c):
        cols = pl.ds(pl.multiple_of(t * TILE, TILE), TILE)
        up = jnp.dot(att[...], wo_all[:, cols], preferred_element_type=jnp.float32)
        h_out[:, cols] = (h_in[:, cols].astype(jnp.float32) + up).astype(jnp.bfloat16)
        return c

    lax.fori_loop(0, d // TILE, out_tile, 0)

    @pl.when(s != last)
    def _():
        h_copy.start()

    def row_copy(i):
        return pltpu.make_async_remote_copy(
            src_ref=h_out.at[pl.ds(i * bucket, bucket)],
            dst_ref=rows_out,
            send_sem=r_send.at[i],
            recv_sem=r_recv,
            device_id=(g, i),
            device_id_type=MESH,
        )

    def stat_copy(i, slot):
        t = lax.rem(me + i, total)
        return pltpu.make_async_remote_copy(
            src_ref=stat,
            dst_ref=stats_all.at[slot],
            send_sem=s_send.at[i],
            recv_sem=s_recv.at[slot],
            device_id=(t // ns, lax.rem(t, ns)),
            device_id_type=MESH,
        )

    def wait_stat(slot):
        stat_copy(1, slot).wait_recv()

    @pl.when(s == last)
    def _():
        for i in range(last):
            row_copy(i).start()
        row_own = pltpu.make_async_copy(
            h_out.at[pl.ds(last * bucket, bucket)], rows_out, r_send.at[last]
        )
        row_own.start()

        t_own.wait()

        def take_term(i, c):
            term_copy(1, lax.rem(me + i, total)).wait_recv()
            return c

        lax.fori_loop(1, total, take_term, 0)

        def add_term(i, acc):
            return acc + term_buf[i].astype(jnp.float32)

        diff_rows = lax.fori_loop(1, total, add_term, term_buf[0].astype(jnp.float32))
        picked = jnp.dot(pick[...], h_out[...], preferred_element_type=jnp.float32)
        readout = rms(picked, final_gain[...]).astype(jnp.float32)
        diffs = jnp.sum(readout * diff_rows, axis=-1, keepdims=True)
        stat[STAT:, :] = jnp.broadcast_to(diffs, (stat.shape[0] - STAT, HD))
        stat[:STAT, :] = jnp.broadcast_to(
            jnp.sum(diffs * cells[...], axis=0, keepdims=True), (STAT, HD)
        )
        s_own = pltpu.make_async_copy(stat, stats_all.at[g], s_send.at[0])
        s_own.start()

        def send_stat(i, c):
            stat_copy(i, g).start()
            return c

        lax.fori_loop(1, total, send_stat, 0)

        def others(i, c):
            wait_stat(lax.rem(g + i, n))
            return c

        lax.fori_loop(1, n, others, 0)

        def sent(i, c):
            stat_copy(i, g).wait_send()
            return c

        lax.fori_loop(1, total, sent, 0)
        s_own.wait()
        row_own.wait()
        for i in range(last):
            row_copy(i).wait_send()

    @pl.when(s != last)
    def _():
        h_copy.wait_send()
        term_copy(0, me).wait_send()
        row_copy(0).wait_recv()

        def every(i, c):
            wait_stat(i)
            return c

        lax.fori_loop(0, n, every, 0)

    def term_sent(i, c):
        term_copy(i, me).wait_send()
        return c

    lax.fori_loop(1, n, term_sent, 0)
    summed = stats_all[0, :STAT, :]
    for k in range(1, n):
        summed = summed + stats_all[k, :STAT, :]
    totals_out[...] = summed
    prompts = diffs_out.shape[0]
    mine = stats_all[g]
    for k in range(ns):

        @pl.when(s == k)
        def _():
            diffs_out[...] = mine[STAT + k * prompts : STAT + (k + 1) * prompts]


def bucket_layout(lengths_rows, seq_len):
    end_rows = jnp.cumsum(lengths_rows, axis=-1).astype(jnp.int32)
    starts = (end_rows - lengths_rows).astype(jnp.int32)
    row_ids = jnp.arange(seq_len, dtype=jnp.int32)
    segment = jnp.sum((row_ids[:, None] >= end_rows[..., None, :]).astype(jnp.int32), axis=-1)
    slots = jnp.arange(lengths_rows.shape[-1], dtype=jnp.int32)
    member = segment[..., :, None] == slots
    position = row_ids - jnp.sum(jnp.where(member, starts[..., None, :], 0), axis=-1)
    return (segment, position, starts)


def per_device(
    n,
    ns,
    embed_in,
    clean_cache,
    lengths,
    patch_layer,
    patch_pos,
    answers,
    attn_gain,
    w_query,
    b_query,
    w_keyval,
    b_key,
    b_value,
    w_out,
    final_gain,
    unembed,
):
    g = lax.axis_index("group")
    s = lax.axis_index("section")
    seq_len, d = embed_in.shape[1:]
    prompts = patch_layer.shape[1]
    entries = lengths.shape[1]
    width = w_query.shape[2]
    kvw = b_key.shape[1]
    rows_all = ns * seq_len
    total = n * ns

    packed = jnp.concatenate(
        [lengths, patch_layer, patch_pos, answers.reshape(1, 2 * prompts)], axis=1
    )
    tile = jnp.pad(packed, ((0, 7), (0, HD - packed.shape[1])))
    table = share(tile, n, ns)[:, 0, : packed.shape[1]]
    at = entries + 2 * prompts
    answer_ids = table[:, at:].reshape(total * prompts, 2)
    mine = lax.dynamic_slice_in_dim(table, g * ns, ns, 0)
    lens = mine[:, :entries]
    layers = mine[:, entries : entries + prompts]
    offsets = mine[:, entries + prompts : at]

    vocab_ids = (g * ns + s) * unembed.shape[0] + jnp.arange(unembed.shape[0], dtype=jnp.int32)
    choosing = (answer_ids[:, 0:1] == vocab_ids[None, :]).astype(jnp.bfloat16) - (
        answer_ids[:, 1:2] == vocab_ids[None, :]
    ).astype(jnp.bfloat16)
    segment, position, starts = bucket_layout(lens, seq_len)
    row_ids = jnp.arange(seq_len, dtype=jnp.int32)
    folded = offsets % lens[:, :prompts]
    target = starts[:, :prompts] + folded
    hit = jnp.any(
        (row_ids[:, None] == target[:, None, :]) & (layers[:, None, :] == s), axis=-1
    )
    hit = hit.reshape(rows_all, 1).astype(jnp.float32)
    ident = (segment + jnp.arange(ns, dtype=jnp.int32)[:, None] * entries).reshape(rows_all)
    all_rows = jnp.arange(rows_all, dtype=jnp.int32)
    mask = (
        (ident[:, None] == ident[None, :]) & (all_rows[None, :] <= all_rows[:, None])
    ).astype(jnp.float32)
    half = HD // 2
    frequency = jnp.exp(jnp.arange(half, dtype=jnp.float32) * (-math.log(ROPE_BASE) / half))
    angles = position.reshape(rows_all, 1).astype(jnp.float32) * frequency[None, :]
    cos_h = jnp.cos(angles)
    sin_h = jnp.sin(angles)
    cosine = jnp.concatenate([cos_h, cos_h], axis=1)
    sinus = jnp.concatenate([-sin_h, sin_h], axis=1)

    ends = starts[:, :prompts] + lens[:, :prompts] - 1
    last_rows = (ends + jnp.arange(ns, dtype=jnp.int32)[:, None] * seq_len).reshape(-1)
    pick = (last_rows[:, None] == all_rows[None, :]).astype(jnp.bfloat16)
    distance = lens[:, :prompts] - 1 - folded
    cell_ids = (layers * MAXLEN + distance).reshape(-1)
    cells = (cell_ids[:, None] == jnp.arange(HD, dtype=jnp.int32)[None, :]).astype(jnp.float32)

    wq, wkv, wo = w_query[0], w_keyval[0], w_out[0]
    ring = n % 2 == 0 and n > 2 and wq.shape[0] % 16 == 0
    if not ring:
        wq, wkv, wo = (lax.all_gather(w, "group", axis=0, tiled=True) for w in (wq, wkv, wo))
    hops = max(n // 2, 1) if ring else 1
    any_ = pl.BlockSpec(memory_space=pl.ANY)
    vmem = pl.BlockSpec(memory_space=pltpu.VMEM)
    dma = pltpu.SemaphoreType.DMA
    stat_rows = STAT + ns * prompts
    rows, totals, diffs = pl.pallas_call(
        functools.partial(window_kernel, n, ns, ring),
        out_shape=(
            jax.ShapeDtypeStruct((seq_len, d), jnp.bfloat16),
            jax.ShapeDtypeStruct((STAT, HD), jnp.float32),
            jax.ShapeDtypeStruct((prompts, HD), jnp.float32),
        ),
        in_specs=[any_] * 5 + [vmem] * 13,
        out_specs=(vmem, vmem, vmem),
        scratch_shapes=[
            pltpu.VMEM((d, width), jnp.bfloat16),
            pltpu.VMEM((d, 2 * kvw), jnp.bfloat16),
            pltpu.VMEM((width, d), jnp.bfloat16),
            pltpu.VMEM((rows_all, d), jnp.bfloat16),
            pltpu.VMEM((rows_all, d), jnp.bfloat16),
            pltpu.VMEM((rows_all, d), jnp.bfloat16),
            pltpu.VMEM((width // HD, rows_all, HD), jnp.bfloat16),
            pltpu.VMEM((kvw // HD, rows_all, HD), jnp.bfloat16),
            pltpu.VMEM((rows_all, kvw), jnp.bfloat16),
            pltpu.VMEM((rows_all, width), jnp.bfloat16),
            pltpu.VMEM((total, ns * prompts, d), jnp.bfloat16),
            pltpu.VMEM((stat_rows, HD), jnp.float32),
            pltpu.VMEM((n, stat_rows, HD), jnp.float32),
            pltpu.VMEM(unembed.shape, jnp.bfloat16),
            pltpu.VMEM((n, ns * prompts, d), jnp.bfloat16),
            dma,
            dma((2, hops, 3)),
            dma((2, hops, 3)),
            dma((3,)),
            dma,
            dma((ns,)),
            dma((n,)),
            dma((total,)),
            dma,
            dma,
            dma,
            dma((ns,)),
            dma,
            dma((total,)),
            dma((n,)),
        ],
        compiler_params=pltpu.CompilerParams(
            collective_id=0, has_side_effects=True, vmem_limit_bytes=60 * 1024 * 1024
        ),
    )(
        embed_in[0],
        wq,
        wkv,
        wo,
        unembed,
        choosing,
        clean_cache[0].reshape(rows_all, d),
        hit,
        mask,
        cosine,
        sinus,
        attn_gain,
        b_query,
        b_key,
        b_value,
        final_gain[None, :],
        pick,
        cells,
    )
    totals = totals[0, : ns * MAXLEN].reshape(ns, MAXLEN)
    return (rows[None], diffs[:, 0][None, :], totals)


def solution(mesh):
    placed = (
        P(("group", "section"), None, None),
        P("section", "group", None, None),
        P(("group", "section"), None),
        P(("group", "section"), None),
        P(("group", "section"), None),
        P(("group", "section"), None, None),
        P("section", None),
        P("section", "group", None),
        P("section", None),
        P("section", "group", None),
        P("section", None),
        P("section", None),
        P("section", "group", None),
        P(),
        P(("group", "section"), None),
    )
    return jax.shard_map(
        functools.partial(per_device, mesh.shape["group"], mesh.shape["section"]),
        mesh=mesh,
        in_specs=placed,
        out_specs=(P(("group", "section"), None, None), P(("group", "section"), None), P()),
        check_vma=False,
    )
```

```python
import functools
import math

import jax
import jax.numpy as jnp
from jax import lax
from jax.experimental import pallas as pl
from jax.experimental.pallas import tpu as pltpu
from jax.sharding import PartitionSpec as P

HD = 128
MAXLEN = 24
EPS = 1e-06
ROPE_BASE = 1000000.0
MESH = pl.DeviceIdType.MESH
TILE = 256
STAT = 8


def rms(rows, gain):
    x = rows.astype(jnp.float32)
    scaled = x * lax.rsqrt(jnp.mean(x * x, axis=-1, keepdims=True) + EPS)
    return (scaled * gain).astype(jnp.bfloat16)


def share_kernel(n, ns, tile, out, send, recv, local):
    g = lax.axis_index("group")
    s = lax.axis_index("section")
    total = n * ns
    me = g * ns + s
    greet_all(me, ns, total)

    def copy(i, slot):
        t = lax.rem(me + i, total)
        return pltpu.make_async_remote_copy(
            src_ref=tile,
            dst_ref=out.at[slot],
            send_sem=send.at[i],
            recv_sem=recv.at[slot],
            device_id=(t // ns, lax.rem(t, ns)),
            device_id_type=MESH,
        )

    def start(i, c):
        copy(i, me).start()
        return c

    def finish(i, c):
        copy(i, lax.rem(me + i, total)).wait_recv()
        return c

    def sent(i, c):
        copy(i, me).wait_send()
        return c

    lax.fori_loop(1, total, start, 0)
    own = pltpu.make_async_copy(tile, out.at[me], local)
    own.start()
    lax.fori_loop(1, total, finish, 0)
    lax.fori_loop(1, total, sent, 0)
    own.wait()


def share(packed, n, ns):
    total = n * ns
    vmem = pl.BlockSpec(memory_space=pltpu.VMEM)
    dma = pltpu.SemaphoreType.DMA
    return pl.pallas_call(
        functools.partial(share_kernel, n, ns),
        out_shape=jax.ShapeDtypeStruct((total,) + packed.shape, packed.dtype),
        in_specs=[vmem],
        out_specs=vmem,
        scratch_shapes=[dma((total,)), dma((total,)), dma],
        compiler_params=pltpu.CompilerParams(collective_id=1, has_side_effects=True),
    )(packed)


def greet_all(me, ns, total):
    barrier = pltpu.get_barrier_semaphore()

    def greet(i, c):
        t = lax.rem(me + i, total)
        pl.semaphore_signal(barrier, inc=1, device_id=(t // ns, lax.rem(t, ns)), device_id_type=MESH)
        return c

    lax.fori_loop(1, total, greet, 0)
    pl.semaphore_wait(barrier, total - 1)


def sliced(n, ns, shard):
    return ns == 4 and n == 2 * ns and shard % 32 == 0


def worker(layer, q, n, ns, by_slice):
    if by_slice:
        return layer * (n // ns) + q // ns, lax.rem(q, ns)
    return q, layer


def role(n, ns, by_slice):
    g = lax.axis_index("group")
    s = lax.axis_index("section")
    if by_slice:
        m = n // ns
        return g // m, lax.rem(g, m) * ns + s
    return s, g


def window_kernel(
    n,
    ns,
    by_slice,
    embed,
    wq,
    wkv,
    wo,
    unembed,
    params,
    clean,
    choose,
    patch_pick,
    place,
    mask,
    cosine,
    sinus,
    final_gain,
    pick,
    cells,
    rows_out,
    totals_out,
    diffs_out,
    wq_all,
    wkv_all,
    wo_all,
    h_in,
    h_out,
    normed,
    q_rot,
    k_rot,
    v_all,
    att,
    term_buf,
    stat,
    stats_all,
    shard_rows,
    terms,
    patches,
    patch_rows,
    layer_params,
    u_sem,
    w_send,
    w_recv,
    w_local,
    f_send,
    e_send,
    e_recv,
    c_send,
    c_recv,
    t_send,
    t_recv,
    h_send,
    h_recv,
    r_send,
    r_recv,
    s_send,
    s_recv,
):
    g = lax.axis_index("group")
    s = lax.axis_index("section")
    total = n * ns
    me = g * ns + s
    last = ns - 1
    layer, q = role(n, ns, by_slice)
    bucket = embed.shape[0]
    d = embed.shape[1]
    width = wq_all.shape[1]
    kvw = wkv_all.shape[1] // 2
    kv_heads = kvw // HD
    heads = width // HD
    per = heads // kv_heads

    def serves(which, group):
        a, b = worker(which, group, n, ns, by_slice)
        return a * ns + b

    def send(src, dst, send_sem, recv_sem, target):
        return pltpu.make_async_remote_copy(
            src_ref=src,
            dst_ref=dst,
            send_sem=send_sem,
            recv_sem=recv_sem,
            device_id=(target // ns, lax.rem(target, ns)),
            device_id_type=MESH,
        )

    def either(target, remote, local):
        pl.when(target != me)(remote)
        pl.when(target == me)(local)

    greet_all(me, ns, total)
    vocab = pltpu.make_async_copy(unembed, shard_rows, u_sem)
    vocab.start()

    ins = (wq, wkv, wo)
    alls = (wq_all, wkv_all, wo_all)
    shard = wq.shape[0]
    if by_slice:
        part = shard // 2
        chunks = [(0, 0, part), (0, part, part), (1, 0, shard), (2, 0, part), (2, part, part)]
        y = lax.rem(g, 2)
        z = g // 2
        x = s // 2
        c = lax.rem(s, 2)

        def span(ch, origin):
            a, first, count = chunks[ch]
            return alls[a].at[pl.ds(pl.multiple_of(origin * shard + first, 16), count)]

        def fresh(ch):
            a, first, count = chunks[ch]
            return ins[a].at[pl.ds(first, count)]

        entry = (s * 2 + y) * ns + x * 2 + lax.rem(z, 2)

        def outward(ch):
            return send(fresh(ch), span(ch, g), w_send.at[ch], w_recv.at[g, ch], entry)

        def homeward(ch):
            return pltpu.make_async_copy(fresh(ch), span(ch, g), w_local.at[ch])

        @pl.when(z != s)
        def _():
            for ch in range(len(chunks)):
                outward(ch).start()

        @pl.when(z == s)
        def _():
            for ch in range(len(chunks)):
                homeward(ch).start()

        side = z // 2
        near = c + 2 * side
        far = c + 2 * (1 - side)
        routes = ((near, y), (far, y), (near, 1 - y), (far, 1 - y))

        def onward(ch, k, way):
            zz, yy = routes[k]
            origin = zz * 2 + yy
            target = (
                g * ns + x * 2 + 1 - c,
                (z * 2 + 1 - y) * ns + s,
                g * ns + (1 - x) * 2 + c,
            )[way]
            return send(
                span(ch, origin), span(ch, origin), f_send.at[k, way, ch], w_recv.at[origin, ch], target
            )

    else:
        local = [pltpu.make_async_copy(ins[a], alls[a], w_local.at[a]) for a in range(3)]
        for copy in local:
            copy.start()

    own_rows = pl.ds(pl.multiple_of(s * bucket, bucket), bucket)
    first = serves(0, g)
    e_out = send(embed, h_in.at[own_rows], e_send, e_recv.at[s], first)
    e_own = pltpu.make_async_copy(embed, h_in.at[own_rows], e_send)
    either(first, e_out.start, e_own.start)
    user = serves(s, g)
    p_out = send(params, layer_params, c_send.at[0], c_recv.at[0], user)
    p_own = pltpu.make_async_copy(params, layer_params, c_send.at[0])
    either(user, p_out.start, p_own.start)
    patches[...] = jnp.dot(
        patch_pick[...], clean[...], preferred_element_type=jnp.float32
    ).astype(jnp.bfloat16)

    vocab.wait()
    block = terms.shape[1]

    def term_tile(t, c):
        cols = pl.ds(pl.multiple_of(t * TILE, TILE), TILE)
        part = jnp.dot(choose[...], shard_rows[:, cols], preferred_element_type=jnp.float32)
        part = part.astype(jnp.bfloat16)
        for k in range(n):
            terms[k, :, cols] = part[k * block : (k + 1) * block]
        return c

    lax.fori_loop(0, d // TILE, term_tile, 0)

    def term_copy(t, slot):
        return send(
            terms.at[t], term_buf.at[slot], t_send.at[t], t_recv.at[slot], serves(last, t)
        )

    def term_own(t):
        return pltpu.make_async_copy(terms.at[t], term_buf.at[me], t_send.at[t])

    def send_term(t, c):
        either(
            serves(last, t),
            lambda: term_copy(t, me).start(),
            lambda: term_own(t).start(),
        )
        return c

    lax.fori_loop(0, n, send_term, 0)
    c_out = send(patches, patch_rows, c_send.at[1], c_recv.at[1], user)
    c_own = pltpu.make_async_copy(patches, patch_rows, c_send.at[1])
    either(user, c_out.start, c_own.start)

    if by_slice:
        for ch in range(len(chunks)):
            for k in range(4):
                if k == 0:

                    @pl.when(z == s)
                    def _():
                        homeward(ch).wait()

                    @pl.when(z != s)
                    def _():
                        onward(ch, 0, 0).wait_recv()

                else:
                    onward(ch, k, 0).wait_recv()
                if k < 2:
                    onward(ch, k, 1).start()

                    @pl.when(x == side)
                    def _():
                        onward(ch, k, 2).start()

                onward(ch, k, 0).start()
        for ch in range(len(chunks)):
            for zz in (1 - c, 3 - c):
                for yy in range(2):
                    origin = zz * 2 + yy
                    send(
                        span(ch, origin), span(ch, origin), w_send.at[ch], w_recv.at[origin, ch], entry
                    ).wait_recv()
    else:
        for copy in local:
            copy.wait()

    tiles = d // TILE

    def h_copy(t):
        cols = pl.ds(pl.multiple_of(t * TILE, TILE), TILE)
        target = serves(lax.rem(layer + 1, ns), q)
        return send(h_out.at[:, cols], h_in.at[:, cols], h_send.at[t], h_recv.at[t], target)

    either(first, lambda: None, e_own.wait)

    @pl.when(layer == 0)
    def _():
        for i in range(ns):

            @pl.when(q * ns + i != me)
            def _():
                rows = pl.ds(i * bucket, bucket)
                send(embed, h_in.at[rows], e_send, e_recv.at[i], first).wait_recv()

    source = q * ns + layer

    @pl.when(source != me)
    def _():
        p_out.wait_recv()
        c_out.wait_recv()

    either(user, lambda: None, p_own.wait)
    either(user, lambda: None, c_own.wait)

    @pl.when(layer != 0)
    def _():
        for t in range(tiles):
            h_copy(t).wait_recv()

    gain = layer_params[:, :d]
    bq = layer_params.at[:, pl.ds(d, width)]
    bk = layer_params[:, d + width : d + width + kvw]
    bv = layer_params[:, d + width + kvw :]

    fill = jnp.dot(place[...], patch_rows[...], preferred_element_type=jnp.float32)
    hit = jnp.sum(place[...].astype(jnp.float32), axis=-1, keepdims=True) > 0
    h_in[...] = jnp.where(hit, fill, h_in[...].astype(jnp.float32)).astype(jnp.bfloat16)
    normed[...] = rms(h_in[...], gain)
    cos_t = cosine[...]
    sin_t = sinus[...]

    def rotate(x):
        return (x * cos_t + pltpu.roll(x, HD // 2, 1) * sin_t).astype(jnp.bfloat16)

    keys = jnp.dot(normed[...], wkv_all[:, :kvw], preferred_element_type=jnp.float32) + bk
    for k in range(kv_heads):
        k_rot[k] = rotate(keys[:, k * HD : (k + 1) * HD])
    values = jnp.dot(normed[...], wkv_all[:, kvw:], preferred_element_type=jnp.float32) + bv
    v_all[...] = values.astype(jnp.bfloat16)

    def query_tile(t, c):
        cols = pl.ds(pl.multiple_of(t * TILE, TILE), TILE)
        q = jnp.dot(normed[...], wq_all[:, cols], preferred_element_type=jnp.float32) + bq[:, cols]
        for k in range(TILE // HD):
            q_rot[t * (TILE // HD) + k] = rotate(q[:, k * HD : (k + 1) * HD])
        return c

    lax.fori_loop(0, width // TILE, query_tile, 0)
    rows_all = h_in.shape[0]
    open_ = mask[...] > 0
    for h in range(heads):
        k = h // per
        sc = lax.dot_general(
            q_rot[h], k_rot[k], (((1,), (1,)), ((), ())), preferred_element_type=jnp.float32
        ) * HD ** (-0.5)
        sc = jnp.where(open_, sc, -1e30)
        ex = jnp.exp(sc - jnp.max(sc, axis=-1, keepdims=True))
        w = (ex / jnp.sum(ex, axis=-1, keepdims=True)).astype(jnp.bfloat16)
        att[:, h * HD : (h + 1) * HD] = jnp.dot(
            w, v_all[:, k * HD : (k + 1) * HD], preferred_element_type=jnp.float32
        ).astype(jnp.bfloat16)

    def out_tile(t, c):
        cols = pl.ds(pl.multiple_of(t * TILE, TILE), TILE)
        up = jnp.dot(att[...], wo_all[:, cols], preferred_element_type=jnp.float32)
        h_out[:, cols] = (h_in[:, cols].astype(jnp.float32) + up).astype(jnp.bfloat16)

        @pl.when((t > 0) & (layer != last))
        def _():
            h_copy(t - 1).start()

        return c

    lax.fori_loop(0, tiles, out_tile, 0)

    @pl.when(layer != last)
    def _():
        h_copy(tiles - 1).start()

    def row_copy(i):
        return send(
            h_out.at[pl.ds(i * bucket, bucket)], rows_out, r_send.at[i], r_recv, q * ns + i
        )

    def row_own(i):
        return pltpu.make_async_copy(
            h_out.at[pl.ds(i * bucket, bucket)], rows_out, r_send.at[i]
        )

    def stat_copy(i, slot):
        t = lax.rem(me + i, total)
        return pltpu.make_async_remote_copy(
            src_ref=stat,
            dst_ref=stats_all.at[slot],
            send_sem=s_send.at[i],
            recv_sem=s_recv.at[slot],
            device_id=(t // ns, lax.rem(t, ns)),
            device_id_type=MESH,
        )

    def wait_stat(slot):
        stat_copy(1, slot).wait_recv()

    @pl.when(layer == last)
    def _():
        for i in range(ns):
            either(q * ns + i, row_copy(i).start, row_own(i).start)
        term_own(q).wait()

        def take_term(i, c):
            term_copy(q, lax.rem(me + i, total)).wait_recv()
            return c

        lax.fori_loop(1, total, take_term, 0)

        def add_term(i, acc):
            return acc + term_buf[i].astype(jnp.float32)

        diff_rows = lax.fori_loop(1, total, add_term, term_buf[0].astype(jnp.float32))
        picked = jnp.dot(pick[...], h_out[...], preferred_element_type=jnp.float32)
        readout = rms(picked, final_gain[...]).astype(jnp.float32)
        diffs = jnp.sum(readout * diff_rows, axis=-1, keepdims=True)
        stat[STAT:, :] = jnp.broadcast_to(diffs, (stat.shape[0] - STAT, HD))
        stat[:STAT, :] = jnp.broadcast_to(
            jnp.sum(diffs * cells[...], axis=0, keepdims=True), (STAT, HD)
        )
        s_own = pltpu.make_async_copy(stat, stats_all.at[q], s_send.at[0])
        s_own.start()

        def send_stat(i, c):
            stat_copy(i, q).start()
            return c

        lax.fori_loop(1, total, send_stat, 0)

        def others(i, c):
            wait_stat(lax.rem(q + i, n))
            return c

        lax.fori_loop(1, n, others, 0)

        def sent(i, c):
            stat_copy(i, q).wait_send()
            return c

        lax.fori_loop(1, total, sent, 0)
        s_own.wait()
        for i in range(ns):
            either(q * ns + i, row_copy(i).wait_send, row_own(i).wait)

    @pl.when(layer != last)
    def _():
        for t in range(tiles):
            h_copy(t).wait_send()

        def every(i, c):
            wait_stat(i)
            return c

        lax.fori_loop(0, n, every, 0)

    @pl.when(serves(last, g) != me)
    def _():
        row_copy(0).wait_recv()

    def term_sent(t, c):
        pl.when(serves(last, t) != me)(lambda: term_copy(t, me).wait_send())
        return c

    lax.fori_loop(0, n, term_sent, 0)
    either(first, e_out.wait_send, lambda: None)
    either(user, p_out.wait_send, lambda: None)
    either(user, c_out.wait_send, lambda: None)
    if by_slice:

        @pl.when(z != s)
        def _():
            for ch in range(len(chunks)):
                outward(ch).wait_send()

        for ch in range(len(chunks)):
            for k in range(4):
                onward(ch, k, 0).wait_send()
                if k < 2:
                    onward(ch, k, 1).wait_send()

                    @pl.when(x == side)
                    def _():
                        onward(ch, k, 2).wait_send()

    summed = stats_all[0, :STAT, :]
    for k in range(1, n):
        summed = summed + stats_all[k, :STAT, :]
    totals_out[...] = summed
    prompts = diffs_out.shape[0]
    mine = stats_all[g]
    for k in range(ns):

        @pl.when(s == k)
        def _():
            diffs_out[...] = mine[STAT + k * prompts : STAT + (k + 1) * prompts]


def bucket_layout(lengths_rows, seq_len):
    end_rows = jnp.cumsum(lengths_rows, axis=-1).astype(jnp.int32)
    starts = (end_rows - lengths_rows).astype(jnp.int32)
    row_ids = jnp.arange(seq_len, dtype=jnp.int32)
    segment = jnp.sum((row_ids[:, None] >= end_rows[..., None, :]).astype(jnp.int32), axis=-1)
    slots = jnp.arange(lengths_rows.shape[-1], dtype=jnp.int32)
    member = segment[..., :, None] == slots
    position = row_ids - jnp.sum(jnp.where(member, starts[..., None, :], 0), axis=-1)
    return (segment, position, starts)


def per_device(
    n,
    ns,
    embed_in,
    clean_cache,
    lengths,
    patch_layer,
    patch_pos,
    answers,
    attn_gain,
    w_query,
    b_query,
    w_keyval,
    b_key,
    b_value,
    w_out,
    final_gain,
    unembed,
):
    g = lax.axis_index("group")
    s = lax.axis_index("section")
    seq_len, d = embed_in.shape[1:]
    prompts = patch_layer.shape[1]
    entries = lengths.shape[1]
    width = w_query.shape[2]
    kvw = b_key.shape[1]
    rows_all = ns * seq_len
    total = n * ns

    packed = jnp.concatenate(
        [lengths, patch_layer, patch_pos, answers.reshape(1, 2 * prompts)], axis=1
    )
    tile = jnp.pad(packed, ((0, 7), (0, HD - packed.shape[1])))
    table = share(tile, n, ns)[:, 0, : packed.shape[1]]
    at = entries + 2 * prompts
    answer_ids = table[:, at:].reshape(total * prompts, 2)
    by_slice = sliced(n, ns, w_query.shape[1])
    layer, q = role(n, ns, by_slice)

    def of_group(which):
        part = lax.dynamic_slice_in_dim(table, which * ns, ns, 0)
        return part[:, :entries], part[:, entries : entries + prompts], part[:, entries + prompts : at]

    def targets(lens, offsets):
        starts = jnp.cumsum(lens, axis=-1) - lens
        folded = offsets % lens[:, :prompts]
        base = jnp.arange(ns, dtype=jnp.int32)[:, None] * seq_len
        return (starts[:, :prompts] + folded + base).reshape(-1)

    lens_g, _, offsets_g = of_group(g)
    lens, layers, offsets = of_group(q)
    vocab_ids = (g * ns + s) * unembed.shape[0] + jnp.arange(unembed.shape[0], dtype=jnp.int32)
    choosing = (answer_ids[:, 0:1] == vocab_ids[None, :]).astype(jnp.bfloat16) - (
        answer_ids[:, 1:2] == vocab_ids[None, :]
    ).astype(jnp.bfloat16)
    segment, position, starts = bucket_layout(lens, seq_len)
    row_ids = jnp.arange(seq_len, dtype=jnp.int32)
    folded = offsets % lens[:, :prompts]
    all_rows = jnp.arange(rows_all, dtype=jnp.int32)
    patch_pick = (targets(lens_g, offsets_g)[:, None] == all_rows[None, :]).astype(jnp.bfloat16)
    place = (
        (all_rows[:, None] == targets(lens, offsets)[None, :])
        & (layers.reshape(1, -1) == layer)
    ).astype(jnp.bfloat16)
    ident = (segment + jnp.arange(ns, dtype=jnp.int32)[:, None] * entries).reshape(rows_all)
    mask = (
        (ident[:, None] == ident[None, :]) & (all_rows[None, :] <= all_rows[:, None])
    ).astype(jnp.float32)
    half = HD // 2
    frequency = jnp.exp(jnp.arange(half, dtype=jnp.float32) * (-math.log(ROPE_BASE) / half))
    angles = position.reshape(rows_all, 1).astype(jnp.float32) * frequency[None, :]
    cos_h = jnp.cos(angles)
    sin_h = jnp.sin(angles)
    cosine = jnp.concatenate([cos_h, cos_h], axis=1)
    sinus = jnp.concatenate([-sin_h, sin_h], axis=1)

    ends = starts[:, :prompts] + lens[:, :prompts] - 1
    last_rows = (ends + jnp.arange(ns, dtype=jnp.int32)[:, None] * seq_len).reshape(-1)
    pick = (last_rows[:, None] == all_rows[None, :]).astype(jnp.bfloat16)
    distance = lens[:, :prompts] - 1 - folded
    cell_ids = (layers * MAXLEN + distance).reshape(-1)
    cells = (cell_ids[:, None] == jnp.arange(HD, dtype=jnp.int32)[None, :]).astype(jnp.float32)

    wq, wkv, wo = w_query[0], w_keyval[0], w_out[0]
    if not by_slice:
        wq, wkv, wo = (lax.all_gather(w, "group", axis=0, tiled=True) for w in (wq, wkv, wo))
    params = jnp.concatenate([attn_gain, b_query, b_key, b_value], axis=1)
    any_ = pl.BlockSpec(memory_space=pl.ANY)
    vmem = pl.BlockSpec(memory_space=pltpu.VMEM)
    dma = pltpu.SemaphoreType.DMA
    stat_rows = STAT + ns * prompts
    rows, totals, diffs = pl.pallas_call(
        functools.partial(window_kernel, n, ns, by_slice),
        out_shape=(
            jax.ShapeDtypeStruct((seq_len, d), jnp.bfloat16),
            jax.ShapeDtypeStruct((STAT, HD), jnp.float32),
            jax.ShapeDtypeStruct((prompts, HD), jnp.float32),
        ),
        in_specs=[any_] * 5 + [vmem] * 11,
        out_specs=(vmem, vmem, vmem),
        scratch_shapes=[
            pltpu.VMEM((d, width), jnp.bfloat16),
            pltpu.VMEM((d, 2 * kvw), jnp.bfloat16),
            pltpu.VMEM((width, d), jnp.bfloat16),
            pltpu.VMEM((rows_all, d), jnp.bfloat16),
            pltpu.VMEM((rows_all, d), jnp.bfloat16),
            pltpu.VMEM((rows_all, d), jnp.bfloat16),
            pltpu.VMEM((width // HD, rows_all, HD), jnp.bfloat16),
            pltpu.VMEM((kvw // HD, rows_all, HD), jnp.bfloat16),
            pltpu.VMEM((rows_all, kvw), jnp.bfloat16),
            pltpu.VMEM((rows_all, width), jnp.bfloat16),
            pltpu.VMEM((total, ns * prompts, d), jnp.bfloat16),
            pltpu.VMEM((stat_rows, HD), jnp.float32),
            pltpu.VMEM((n, stat_rows, HD), jnp.float32),
            pltpu.VMEM(unembed.shape, jnp.bfloat16),
            pltpu.VMEM((n, ns * prompts, d), jnp.bfloat16),
            pltpu.VMEM((ns * prompts, d), jnp.bfloat16),
            pltpu.VMEM((ns * prompts, d), jnp.bfloat16),
            pltpu.VMEM(params.shape, jnp.float32),
            dma,
            dma((5,)),
            dma((n, 5)),
            dma((5,)),
            dma((4, 3, 5)),
            dma,
            dma((ns,)),
            dma((2,)),
            dma((2,)),
            dma((n,)),
            dma((total,)),
            dma((d // TILE,)),
            dma((d // TILE,)),
            dma((ns,)),
            dma,
            dma((total,)),
            dma((n,)),
        ],
        compiler_params=pltpu.CompilerParams(
            collective_id=0, has_side_effects=True, vmem_limit_bytes=60 * 1024 * 1024
        ),
    )(
        embed_in[0],
        wq,
        wkv,
        wo,
        unembed,
        params,
        clean_cache[0].reshape(rows_all, d),
        choosing,
        patch_pick,
        place,
        mask,
        cosine,
        sinus,
        final_gain[None, :],
        pick,
        cells,
    )
    totals = totals[0, : ns * MAXLEN].reshape(ns, MAXLEN)
    return (rows[None], diffs[:, 0][None, :], totals)


def solution(mesh):
    placed = (
        P(("group", "section"), None, None),
        P("section", "group", None, None),
        P(("group", "section"), None),
        P(("group", "section"), None),
        P(("group", "section"), None),
        P(("group", "section"), None, None),
        P("section", None),
        P("section", "group", None),
        P("section", None),
        P("section", "group", None),
        P("section", None),
        P("section", None),
        P("section", "group", None),
        P(),
        P(("group", "section"), None),
    )
    return jax.shard_map(
        functools.partial(per_device, mesh.shape["group"], mesh.shape["section"]),
        mesh=mesh,
        in_specs=placed,
        out_specs=(P(("group", "section"), None, None), P(("group", "section"), None), P()),
        check_vma=False,
    )
```

```python
import functools
import math

import jax
import jax.numpy as jnp
from jax import lax
from jax.experimental import pallas as pl
from jax.experimental.pallas import tpu as pltpu
from jax.sharding import PartitionSpec as P

HD = 128
MAXLEN = 24
EPS = 1e-06
ROPE_BASE = 1000000.0
MESH = pl.DeviceIdType.MESH
TILE = 256
STAT = 8


def rms(rows, gain):
    x = rows.astype(jnp.float32)
    scaled = x * lax.rsqrt(jnp.mean(x * x, axis=-1, keepdims=True) + EPS)
    return (scaled * gain).astype(jnp.bfloat16)


def share_kernel(n, ns, tile, out, send, recv, local):
    g = lax.axis_index("group")
    s = lax.axis_index("section")
    total = n * ns
    me = g * ns + s
    greet_all(me, ns, total)

    def copy(i, slot):
        t = lax.rem(me + i, total)
        return pltpu.make_async_remote_copy(
            src_ref=tile,
            dst_ref=out.at[slot],
            send_sem=send.at[i],
            recv_sem=recv.at[slot],
            device_id=(t // ns, lax.rem(t, ns)),
            device_id_type=MESH,
        )

    def start(i, c):
        copy(i, me).start()
        return c

    def finish(i, c):
        copy(i, lax.rem(me + i, total)).wait_recv()
        return c

    def sent(i, c):
        copy(i, me).wait_send()
        return c

    lax.fori_loop(1, total, start, 0)
    own = pltpu.make_async_copy(tile, out.at[me], local)
    own.start()
    lax.fori_loop(1, total, finish, 0)
    lax.fori_loop(1, total, sent, 0)
    own.wait()


def share(packed, n, ns):
    total = n * ns
    vmem = pl.BlockSpec(memory_space=pltpu.VMEM)
    dma = pltpu.SemaphoreType.DMA
    return pl.pallas_call(
        functools.partial(share_kernel, n, ns),
        out_shape=jax.ShapeDtypeStruct((total,) + packed.shape, packed.dtype),
        in_specs=[vmem],
        out_specs=vmem,
        scratch_shapes=[dma((total,)), dma((total,)), dma],
        compiler_params=pltpu.CompilerParams(collective_id=1, has_side_effects=True),
    )(packed)


def greet_all(me, ns, total):
    barrier = pltpu.get_barrier_semaphore()

    def greet(i, c):
        t = lax.rem(me + i, total)
        pl.semaphore_signal(barrier, inc=1, device_id=(t // ns, lax.rem(t, ns)), device_id_type=MESH)
        return c

    lax.fori_loop(1, total, greet, 0)
    pl.semaphore_wait(barrier, total - 1)


def ring_group(place, n):
    late = place // (n // 2)
    return (1 - late) * 2 * place + late * (2 * (n - 1 - place) + 1)


def window_kernel(
    n,
    ns,
    ring,
    embed,
    wq,
    wkv,
    wo,
    unembed,
    choose,
    clean,
    hit,
    mask,
    cosine,
    sinus,
    gain,
    bq,
    bk,
    bv,
    final_gain,
    pick,
    cells,
    rows_out,
    totals_out,
    diffs_out,
    wq_all,
    wkv_all,
    wo_all,
    h_in,
    h_out,
    normed,
    q_rot,
    k_rot,
    v_all,
    att,
    term_buf,
    stat,
    stats_all,
    shard_rows,
    terms,
    u_sem,
    w_send,
    w_recv,
    w_local,
    e_send,
    e_recv,
    t_send,
    t_recv,
    t_local,
    h_send,
    h_recv,
    r_send,
    r_recv,
    s_send,
    s_recv,
):
    g = lax.axis_index("group")
    s = lax.axis_index("section")
    total = n * ns
    me = g * ns + s
    last = ns - 1
    bucket = embed.shape[0]
    d = embed.shape[1]
    width = wq_all.shape[1]
    kvw = wkv_all.shape[1] // 2
    kv_heads = kvw // HD
    heads = width // HD
    per = heads // kv_heads

    greet_all(me, ns, total)
    vocab = pltpu.make_async_copy(unembed, shard_rows, u_sem)
    vocab.start()

    ins = (wq, wkv, wo)
    alls = (wq_all, wkv_all, wo_all)
    shard = wq.shape[0]
    if ring:
        odd = lax.rem(g, 2)
        place = (1 - odd) * (g // 2) + odd * (n - 1 - g // 2)
        right = ring_group(lax.rem(place + 1, n), n)
        left = ring_group(lax.rem(place + n - 1, n), n)
        half = n // 2

        def rows_of(step, way):
            at = lax.rem(place + n - step, n) if way == 0 else lax.rem(place + step, n)
            return pl.ds(pl.multiple_of(ring_group(at, n) * shard, shard), shard)

        def hop(step, way, a):
            rows = rows_of(step, way)
            src = ins[a] if step == 0 else alls[a].at[rows]
            return pltpu.make_async_remote_copy(
                src_ref=src,
                dst_ref=alls[a].at[rows],
                send_sem=w_send.at[way, step, a],
                recv_sem=w_recv.at[way, step, a],
                device_id=((right, left)[way], s),
                device_id_type=MESH,
            )

        def used(step, way, a):
            if step < half - 1:
                return True
            return (a == 0) if way == 0 else (a != 0)

        for a in range(3):
            for way in range(2):
                if used(0, way, a):
                    hop(0, way, a).start()
        own = pl.ds(pl.multiple_of(g * shard, shard), shard)
    else:
        own = pl.ds(0, shard)
    local = [
        pltpu.make_async_copy(ins[a], alls[a].at[own], w_local.at[a]) for a in range(3)
    ]
    for copy in local:
        copy.start()

    own_rows = pl.ds(pl.multiple_of(s * bucket, bucket), bucket)
    e_out = pltpu.make_async_remote_copy(
        src_ref=embed,
        dst_ref=h_in.at[own_rows],
        send_sem=e_send,
        recv_sem=e_recv.at[s],
        device_id=(g, 0),
        device_id_type=MESH,
    )
    e_own = pltpu.make_async_copy(embed, h_in.at[own_rows], e_send)

    @pl.when(s != 0)
    def _():
        e_out.start()

    @pl.when(s == 0)
    def _():
        e_own.start()

    vocab.wait()
    block = terms.shape[1]

    def term_tile(t, c):
        cols = pl.ds(pl.multiple_of(t * TILE, TILE), TILE)
        part = jnp.dot(choose[...], shard_rows[:, cols], preferred_element_type=jnp.float32)
        part = part.astype(jnp.bfloat16)
        for k in range(n):
            terms[k, :, cols] = part[k * block : (k + 1) * block]
        return c

    lax.fori_loop(0, d // TILE, term_tile, 0)

    def term_copy(i, slot):
        t = lax.rem(g + i, n)
        return pltpu.make_async_remote_copy(
            src_ref=terms.at[t],
            dst_ref=term_buf.at[slot],
            send_sem=t_send.at[i],
            recv_sem=t_recv.at[slot],
            device_id=(t, last),
            device_id_type=MESH,
        )

    def send_term(i, c):
        term_copy(i, me).start()
        return c

    if ring:
        for step in range(1, half):
            for a in range(3):
                for way in range(2):
                    hop(step - 1, way, a).wait_recv()
                    if used(step, way, a):
                        hop(step, way, a).start()
        for a in range(3):
            for way in range(2):
                if used(half - 1, way, a):
                    hop(half - 1, way, a).wait_recv()
        for step in range(half):
            for a in range(3):
                for way in range(2):
                    if used(step, way, a):
                        hop(step, way, a).wait_send()
    for copy in local:
        copy.wait()

    t_own = pltpu.make_async_copy(terms.at[g], term_buf.at[me], t_local)

    @pl.when(s == last)
    def _():
        t_own.start()

    @pl.when(s != last)
    def _():
        term_copy(0, me).start()

    lax.fori_loop(1, n, send_term, 0)

    tiles = d // TILE

    def h_copy(t):
        cols = pl.ds(pl.multiple_of(t * TILE, TILE), TILE)
        return pltpu.make_async_remote_copy(
            src_ref=h_out.at[:, cols],
            dst_ref=h_in.at[:, cols],
            send_sem=h_send.at[t],
            recv_sem=h_recv.at[t],
            device_id=(g, lax.rem(s + 1, ns)),
            device_id_type=MESH,
        )

    @pl.when(s == 0)
    def _():
        e_own.wait()
        for i in range(1, ns):
            rows = pl.ds(i * bucket, bucket)
            pltpu.make_async_remote_copy(
                src_ref=embed,
                dst_ref=h_in.at[rows],
                send_sem=e_send,
                recv_sem=e_recv.at[i],
                device_id=(g, 0),
                device_id_type=MESH,
            ).wait_recv()

    @pl.when(s != 0)
    def _():
        e_out.wait_send()
        for t in range(tiles):
            h_copy(t).wait_recv()

    h_in[...] = jnp.where(hit[...] > 0, clean[...], h_in[...])
    normed[...] = rms(h_in[...], gain[...])
    cos_t = cosine[...]
    sin_t = sinus[...]

    def rotate(x):
        return (x * cos_t + pltpu.roll(x, HD // 2, 1) * sin_t).astype(jnp.bfloat16)

    keys = jnp.dot(normed[...], wkv_all[:, :kvw], preferred_element_type=jnp.float32) + bk[...]
    for k in range(kv_heads):
        k_rot[k] = rotate(keys[:, k * HD : (k + 1) * HD])
    values = jnp.dot(normed[...], wkv_all[:, kvw:], preferred_element_type=jnp.float32) + bv[...]
    v_all[...] = values.astype(jnp.bfloat16)

    def query_tile(t, c):
        cols = pl.ds(pl.multiple_of(t * TILE, TILE), TILE)
        q = jnp.dot(normed[...], wq_all[:, cols], preferred_element_type=jnp.float32) + bq[:, cols]
        for k in range(TILE // HD):
            q_rot[t * (TILE // HD) + k] = rotate(q[:, k * HD : (k + 1) * HD])
        return c

    lax.fori_loop(0, width // TILE, query_tile, 0)
    rows_all = h_in.shape[0]
    open_ = mask[...] > 0
    for h in range(heads):
        k = h // per
        sc = lax.dot_general(
            q_rot[h], k_rot[k], (((1,), (1,)), ((), ())), preferred_element_type=jnp.float32
        ) * HD ** (-0.5)
        sc = jnp.where(open_, sc, -1e30)
        ex = jnp.exp(sc - jnp.max(sc, axis=-1, keepdims=True))
        w = (ex / jnp.sum(ex, axis=-1, keepdims=True)).astype(jnp.bfloat16)
        att[:, h * HD : (h + 1) * HD] = jnp.dot(
            w, v_all[:, k * HD : (k + 1) * HD], preferred_element_type=jnp.float32
        ).astype(jnp.bfloat16)

    def out_tile(t, c):
        cols = pl.ds(pl.multiple_of(t * TILE, TILE), TILE)
        up = jnp.dot(att[...], wo_all[:, cols], preferred_element_type=jnp.float32)
        h_out[:, cols] = (h_in[:, cols].astype(jnp.float32) + up).astype(jnp.bfloat16)

        @pl.when((t > 0) & (s != last))
        def _():
            h_copy(t - 1).start()

        return c

    lax.fori_loop(0, tiles, out_tile, 0)

    @pl.when(s != last)
    def _():
        h_copy(tiles - 1).start()

    def row_copy(i):
        return pltpu.make_async_remote_copy(
            src_ref=h_out.at[pl.ds(i * bucket, bucket)],
            dst_ref=rows_out,
            send_sem=r_send.at[i],
            recv_sem=r_recv,
            device_id=(g, i),
            device_id_type=MESH,
        )

    def stat_copy(i, slot):
        t = lax.rem(me + i, total)
        return pltpu.make_async_remote_copy(
            src_ref=stat,
            dst_ref=stats_all.at[slot],
            send_sem=s_send.at[i],
            recv_sem=s_recv.at[slot],
            device_id=(t // ns, lax.rem(t, ns)),
            device_id_type=MESH,
        )

    def wait_stat(slot):
        stat_copy(1, slot).wait_recv()

    @pl.when(s == last)
    def _():
        for i in range(last):
            row_copy(i).start()
        row_own = pltpu.make_async_copy(
            h_out.at[pl.ds(last * bucket, bucket)], rows_out, r_send.at[last]
        )
        row_own.start()

        t_own.wait()

        def take_term(i, c):
            term_copy(1, lax.rem(me + i, total)).wait_recv()
            return c

        lax.fori_loop(1, total, take_term, 0)

        def add_term(i, acc):
            return acc + term_buf[i].astype(jnp.float32)

        diff_rows = lax.fori_loop(1, total, add_term, term_buf[0].astype(jnp.float32))
        picked = jnp.dot(pick[...], h_out[...], preferred_element_type=jnp.float32)
        readout = rms(picked, final_gain[...]).astype(jnp.float32)
        diffs = jnp.sum(readout * diff_rows, axis=-1, keepdims=True)
        stat[STAT:, :] = jnp.broadcast_to(diffs, (stat.shape[0] - STAT, HD))
        stat[:STAT, :] = jnp.broadcast_to(
            jnp.sum(diffs * cells[...], axis=0, keepdims=True), (STAT, HD)
        )
        s_own = pltpu.make_async_copy(stat, stats_all.at[g], s_send.at[0])
        s_own.start()

        def send_stat(i, c):
            stat_copy(i, g).start()
            return c

        lax.fori_loop(1, total, send_stat, 0)

        def others(i, c):
            wait_stat(lax.rem(g + i, n))
            return c

        lax.fori_loop(1, n, others, 0)

        def sent(i, c):
            stat_copy(i, g).wait_send()
            return c

        lax.fori_loop(1, total, sent, 0)
        s_own.wait()
        row_own.wait()
        for i in range(last):
            row_copy(i).wait_send()

    @pl.when(s != last)
    def _():
        for t in range(tiles):
            h_copy(t).wait_send()
        term_copy(0, me).wait_send()
        row_copy(0).wait_recv()

        def every(i, c):
            wait_stat(i)
            return c

        lax.fori_loop(0, n, every, 0)

    def term_sent(i, c):
        term_copy(i, me).wait_send()
        return c

    lax.fori_loop(1, n, term_sent, 0)
    summed = stats_all[0, :STAT, :]
    for k in range(1, n):
        summed = summed + stats_all[k, :STAT, :]
    totals_out[...] = summed
    prompts = diffs_out.shape[0]
    mine = stats_all[g]
    for k in range(ns):

        @pl.when(s == k)
        def _():
            diffs_out[...] = mine[STAT + k * prompts : STAT + (k + 1) * prompts]


def bucket_layout(lengths_rows, seq_len):
    end_rows = jnp.cumsum(lengths_rows, axis=-1).astype(jnp.int32)
    starts = (end_rows - lengths_rows).astype(jnp.int32)
    row_ids = jnp.arange(seq_len, dtype=jnp.int32)
    segment = jnp.sum((row_ids[:, None] >= end_rows[..., None, :]).astype(jnp.int32), axis=-1)
    slots = jnp.arange(lengths_rows.shape[-1], dtype=jnp.int32)
    member = segment[..., :, None] == slots
    position = row_ids - jnp.sum(jnp.where(member, starts[..., None, :], 0), axis=-1)
    return (segment, position, starts)


def per_device(
    n,
    ns,
    embed_in,
    clean_cache,
    lengths,
    patch_layer,
    patch_pos,
    answers,
    attn_gain,
    w_query,
    b_query,
    w_keyval,
    b_key,
    b_value,
    w_out,
    final_gain,
    unembed,
):
    g = lax.axis_index("group")
    s = lax.axis_index("section")
    seq_len, d = embed_in.shape[1:]
    prompts = patch_layer.shape[1]
    entries = lengths.shape[1]
    width = w_query.shape[2]
    kvw = b_key.shape[1]
    rows_all = ns * seq_len
    total = n * ns

    packed = jnp.concatenate(
        [lengths, patch_layer, patch_pos, answers.reshape(1, 2 * prompts)], axis=1
    )
    tile = jnp.pad(packed, ((0, 7), (0, HD - packed.shape[1])))
    table = share(tile, n, ns)[:, 0, : packed.shape[1]]
    at = entries + 2 * prompts
    answer_ids = table[:, at:].reshape(total * prompts, 2)
    mine = lax.dynamic_slice_in_dim(table, g * ns, ns, 0)
    lens = mine[:, :entries]
    layers = mine[:, entries : entries + prompts]
    offsets = mine[:, entries + prompts : at]

    vocab_ids = (g * ns + s) * unembed.shape[0] + jnp.arange(unembed.shape[0], dtype=jnp.int32)
    choosing = (answer_ids[:, 0:1] == vocab_ids[None, :]).astype(jnp.bfloat16) - (
        answer_ids[:, 1:2] == vocab_ids[None, :]
    ).astype(jnp.bfloat16)
    segment, position, starts = bucket_layout(lens, seq_len)
    row_ids = jnp.arange(seq_len, dtype=jnp.int32)
    folded = offsets % lens[:, :prompts]
    target = starts[:, :prompts] + folded
    hit = jnp.any(
        (row_ids[:, None] == target[:, None, :]) & (layers[:, None, :] == s), axis=-1
    )
    hit = hit.reshape(rows_all, 1).astype(jnp.float32)
    ident = (segment + jnp.arange(ns, dtype=jnp.int32)[:, None] * entries).reshape(rows_all)
    all_rows = jnp.arange(rows_all, dtype=jnp.int32)
    mask = (
        (ident[:, None] == ident[None, :]) & (all_rows[None, :] <= all_rows[:, None])
    ).astype(jnp.float32)
    half = HD // 2
    frequency = jnp.exp(jnp.arange(half, dtype=jnp.float32) * (-math.log(ROPE_BASE) / half))
    angles = position.reshape(rows_all, 1).astype(jnp.float32) * frequency[None, :]
    cos_h = jnp.cos(angles)
    sin_h = jnp.sin(angles)
    cosine = jnp.concatenate([cos_h, cos_h], axis=1)
    sinus = jnp.concatenate([-sin_h, sin_h], axis=1)

    ends = starts[:, :prompts] + lens[:, :prompts] - 1
    last_rows = (ends + jnp.arange(ns, dtype=jnp.int32)[:, None] * seq_len).reshape(-1)
    pick = (last_rows[:, None] == all_rows[None, :]).astype(jnp.bfloat16)
    distance = lens[:, :prompts] - 1 - folded
    cell_ids = (layers * MAXLEN + distance).reshape(-1)
    cells = (cell_ids[:, None] == jnp.arange(HD, dtype=jnp.int32)[None, :]).astype(jnp.float32)

    wq, wkv, wo = w_query[0], w_keyval[0], w_out[0]
    ring = n % 2 == 0 and n > 2 and wq.shape[0] % 16 == 0
    if not ring:
        wq, wkv, wo = (lax.all_gather(w, "group", axis=0, tiled=True) for w in (wq, wkv, wo))
    hops = max(n // 2, 1) if ring else 1
    any_ = pl.BlockSpec(memory_space=pl.ANY)
    vmem = pl.BlockSpec(memory_space=pltpu.VMEM)
    dma = pltpu.SemaphoreType.DMA
    stat_rows = STAT + ns * prompts
    rows, totals, diffs = pl.pallas_call(
        functools.partial(window_kernel, n, ns, ring),
        out_shape=(
            jax.ShapeDtypeStruct((seq_len, d), jnp.bfloat16),
            jax.ShapeDtypeStruct((STAT, HD), jnp.float32),
            jax.ShapeDtypeStruct((prompts, HD), jnp.float32),
        ),
        in_specs=[any_] * 5 + [vmem] * 13,
        out_specs=(vmem, vmem, vmem),
        scratch_shapes=[
            pltpu.VMEM((d, width), jnp.bfloat16),
            pltpu.VMEM((d, 2 * kvw), jnp.bfloat16),
            pltpu.VMEM((width, d), jnp.bfloat16),
            pltpu.VMEM((rows_all, d), jnp.bfloat16),
            pltpu.VMEM((rows_all, d), jnp.bfloat16),
            pltpu.VMEM((rows_all, d), jnp.bfloat16),
            pltpu.VMEM((width // HD, rows_all, HD), jnp.bfloat16),
            pltpu.VMEM((kvw // HD, rows_all, HD), jnp.bfloat16),
            pltpu.VMEM((rows_all, kvw), jnp.bfloat16),
            pltpu.VMEM((rows_all, width), jnp.bfloat16),
            pltpu.VMEM((total, ns * prompts, d), jnp.bfloat16),
            pltpu.VMEM((stat_rows, HD), jnp.float32),
            pltpu.VMEM((n, stat_rows, HD), jnp.float32),
            pltpu.VMEM(unembed.shape, jnp.bfloat16),
            pltpu.VMEM((n, ns * prompts, d), jnp.bfloat16),
            dma,
            dma((2, hops, 3)),
            dma((2, hops, 3)),
            dma((3,)),
            dma,
            dma((ns,)),
            dma((n,)),
            dma((total,)),
            dma,
            dma((d // TILE,)),
            dma((d // TILE,)),
            dma((ns,)),
            dma,
            dma((total,)),
            dma((n,)),
        ],
        compiler_params=pltpu.CompilerParams(
            collective_id=0, has_side_effects=True, vmem_limit_bytes=60 * 1024 * 1024
        ),
    )(
        embed_in[0],
        wq,
        wkv,
        wo,
        unembed,
        choosing,
        clean_cache[0].reshape(rows_all, d),
        hit,
        mask,
        cosine,
        sinus,
        attn_gain,
        b_query,
        b_key,
        b_value,
        final_gain[None, :],
        pick,
        cells,
    )
    totals = totals[0, : ns * MAXLEN].reshape(ns, MAXLEN)
    return (rows[None], diffs[:, 0][None, :], totals)


def solution(mesh):
    placed = (
        P(("group", "section"), None, None),
        P("section", "group", None, None),
        P(("group", "section"), None),
        P(("group", "section"), None),
        P(("group", "section"), None),
        P(("group", "section"), None, None),
        P("section", None),
        P("section", "group", None),
        P("section", None),
        P("section", "group", None),
        P("section", None),
        P("section", None),
        P("section", "group", None),
        P(),
        P(("group", "section"), None),
    )
    return jax.shard_map(
        functools.partial(per_device, mesh.shape["group"], mesh.shape["section"]),
        mesh=mesh,
        in_specs=placed,
        out_specs=(P(("group", "section"), None, None), P(("group", "section"), None), P()),
        check_vma=False,
    )
```
